256 devices in a mesh: expert: 16 (over y_lo, x, core), dp: 16 (over y_hi, z).
Axes of the slice: x: 4, y: 4 (y_hi: 2, y_lo: 2; y = y_hi * 2 + y_lo), z: 8, core: 2. Of those that a mesh axis runs over, the one named last changes fastest.
Arguments:
- attn_input: bfloat16 [12288, 4096], P('dp'), may hold values from -6 to 6
- query_grad: bfloat16 [12288, 8192], P('dp', 'expert'), may hold values from -6 to 6
- query_weight: float32 [8192, 4096], P(('expert', 'dp')), may hold values from -40 to 40
- moe_cotangent: bfloat16 [2048, 4096], P('expert', 'dp'), may hold values from -6 to 6
- expert_ids: int32 [2048, 8], P('expert'), may hold values from 0 to 31, all different within a row; in each aligned block of 128 rows (0 to 127, 128 to 255, ...) at most 40 rows name the same one
- route_weights: float32 [2048, 8], P('expert'), may hold values from 0.2 to 1
- gate_saved: bfloat16 [640, 32, 1536], P('dp', 'expert'), may hold values from -6 to 6
- up_saved: bfloat16 [640, 32, 1536], P('dp', 'expert'), may hold values from -6 to 6
- gate_weight: bfloat16 [32, 4096, 1536], P('expert', 'dp'), may hold values from -0.09375 to 0.09375
- up_weight: bfloat16 [32, 4096, 1536], P('expert', 'dp'), may hold values from -0.09375 to 0.09375
- down_weight: bfloat16 [32, 1536, 4096], P('expert', None, 'dp'), may hold values from -0.15625 to 0.15625
Outputs:
- query_weight_next: float32 [8192, 4096], P(('expert', 'dp'))
- moe_input_grad: float32 [2048, 4096], P('expert', 'dp')
The draws below stay inside these ranges and needn't reach their ends.
Inputs may be any that keep to these rules, and one draw needn't show every extreme that they name: `expert_ids`: in each aligned block of 128 rows no expert is named by more than 40 rows, and one expert by exactly 40 rows in some block; each row names 8 different experts.
All inputs are finite; a program needn't handle non-finite values.
Results may differ from the reference program's by a relative error of at most 0.022.
Values may be sent and summed in bfloat16 or wider, within the bound.
A program may use at most 128 MiB of HBM per device.

```python
import math
import jax
import jax.numpy as jnp
import numpy as np
from jax import lax

D = 4096
FF = 1536
TOPK = 8
TOK_ATT = 768
TOK_MOE = 128
EXPERTS = 32
CAP = 40
SLOTS = 640
QCOLS = 8192
TOKENS_ATT = 12288
MOE_ROWS = 2048
N_EXPERT = 16
N_DP = 16


def draw_query_weight(key, part):
    first_key = jax.random.fold_in(key, 11)
    row_key = jax.random.fold_in(key, 12)
    column_key = jax.random.fold_in(key, 13)
    base = jnp.clip(jax.random.normal(first_key, (QCOLS, D), jnp.float32), -4.0, 4.0)
    row_scale = jnp.exp(jax.random.uniform(row_key, (QCOLS, 1), jnp.float32, 0.0, math.log(10.0)))
    column_scale = jnp.exp(jax.random.uniform(column_key, (1, D), jnp.float32, 0.0, math.log(10.0)))
    return base * row_scale * column_scale * 0.1


def strengthened(entries, stream_key, source, target, shards_of, factor):
    owner, partner = [(jnp.arange(entries.shape[dim]) // (entries.shape[dim] // shards_of)).reshape([-1 if axis == dim else 1 for axis in range(entries.ndim)]) for dim in (source, target)]
    chosen = jax.random.permutation(stream_key, shards_of)[partner]
    strong = (owner == chosen) | (owner == (partner + shards_of // 2) % shards_of)
    return jnp.where(strong, factor * entries, entries)


def level_of(key, dims, shards, low, top_value):
    def one(axis_at, parts):
        heights = jax.random.uniform(jax.random.fold_in(jax.random.fold_in(key, 6), axis_at), (parts,), jnp.float32, low / len(shards), top_value / len(shards))
        return jnp.repeat(jnp.exp(heights), dims[axis_at] // parts).reshape((-1,) + (1,) * (len(dims) - axis_at - 1))

    loudness = one(*shards[0])
    for cut in shards[1:]:
        loudness = loudness * one(*cut)
    return loudness


def routed_block(key, own, number, rows, count, top, limit, skew):
    ranking = jax.random.permutation(key, count)
    heavy_load, usual = portions_of(count, rows * top, limit, skew, True), portions_of(count, rows * top, limit, skew, False)
    places = jnp.arange(count)

    def named(sizes, rotation):
        used = int((sizes > 0).sum())
        fixed = max(1, used // 4)
        shifted = fixed + (places - fixed + rotation * (used - fixed)) % max(1, count - fixed)
        return jnp.zeros((count,), jnp.int32).at[ranking[jnp.where(places < fixed, places, shifted)]].set(jnp.asarray(sizes, jnp.int32))

    sizes = jnp.where(number % 4 == 0, named(heavy_load, number // 4), named(usual, number - number // 4 - 1))
    mixed = jax.random.permutation(jax.random.fold_in(own, 3), count)
    giver, taker = mixed[0:count // 2 * 2:2], mixed[1:count // 2 * 2:2]
    slack = jnp.minimum(sizes[giver] - 1, limit - sizes[taker]) // 2
    slack = jnp.where((giver == ranking[0]) | (taker == ranking[0]) | (sizes[taker] == 0), 0, jnp.maximum(slack, 0))
    shifted = jax.random.randint(jax.random.fold_in(own, 4), (count // 2,), 0, 1 << 20) % (slack + 1)
    sizes = sizes.at[giver].add(-shifted).at[taker].add(shifted)
    labels = jnp.searchsorted(jnp.cumsum(sizes), jnp.arange(rows * top), side="right").astype(jnp.int32)
    listing = labels.reshape(top, rows).T
    listing = listing[jax.random.permutation(jax.random.fold_in(own, 1), rows)]
    rotation = jax.random.randint(jax.random.fold_in(own, 2), (rows, 1), 0, top)
    return jnp.take_along_axis(listing, (jnp.arange(top)[None, :] + rotation) % top, axis=1)


def portions_of(count, total, reach, lean, full):
    loads = [(1 << 20) // math.isqrt(standing ** lean) + 1 for standing in range(1, count + 1)]
    largest = reach if full else min(reach, max(-(-total // count), total * loads[0] // sum(loads)))
    least = 1 if total - largest >= count - 1 else 0
    holding, rest = [largest] + [least] * (count - 1), total - largest - least * (count - 1)
    while rest > 0:
        movable = [i for i in range(1, count) if holding[i] < largest] or [i for i in range(1, count) if holding[i] < reach]
        pool, left = sum([loads[i] for i in movable]), rest
        for i in movable:
            addition = min(reach - holding[i], max(1, left * loads[i] // pool), rest)
            holding[i] = holding[i] + addition
            rest = rest - addition
    return np.array(holding)


def gaussian(key, extent, scale, bound, cuts=(), kind=jnp.bfloat16):
    level = level_of(key, extent, cuts, -0.22, 0.18) if cuts else 1.0
    entries = jax.random.normal(key, extent, jnp.float32) * scale * level
    return jnp.minimum(jnp.maximum(entries, -bound), bound).astype(kind)


def noise_with(own_key, dims, spread, bound, split, heavy, kind=jnp.bfloat16):
    array = spread * jax.random.normal(own_key, dims, jnp.float32)
    if split:
        array = array * level_of(own_key, dims, split, -0.22, 0.18)
    return jnp.clip(strengthened(array, jax.random.fold_in(own_key, 3), *heavy), -bound, bound).astype(kind)


def setup_inputs(seed: int = 0) -> dict:
    key_list = jax.random.split(jax.random.key(seed), 12)
    attn_input = gaussian(key_list[0], (TOKENS_ATT, D), 1.0, 6.0, ((0, 16),))
    query_grad = noise_with(key_list[1], (TOKENS_ATT, QCOLS), 1.0, 6.0, ((0, 16), (1, 16)), (0, 1, 16, 2.0))
    query_weight = draw_query_weight(jax.random.fold_in(key_list[11], 71), 0)
    moe_cotangent = gaussian(key_list[3], (MOE_ROWS, D), 1.0, 6.0, ((0, 16), (1, 16)))
    expert_ids_keys = jax.random.split(jax.random.fold_in(key_list[4], 1), MOE_ROWS // TOK_MOE)
    expert_ids_turns = jax.random.permutation(jax.random.fold_in(key_list[4], 3), MOE_ROWS // TOK_MOE)
    expert_ids = jax.vmap(lambda own, number: routed_block(jax.random.fold_in(key_list[4], 2), own, number, TOK_MOE, EXPERTS, TOPK, CAP, 1))(expert_ids_keys, expert_ids_turns).reshape((MOE_ROWS, TOPK))
    route_weights = jnp.clip(0.2 + 0.8 * jax.random.uniform(key_list[5], (MOE_ROWS, TOPK), jnp.float32) ** level_of(key_list[5], (MOE_ROWS, TOPK), ((0, 16),), -0.2, 0.2), 0.2, 1.0)
    gate_saved = gaussian(key_list[6], (SLOTS, EXPERTS, FF), 1.0, 6.0, ((0, 16), (1, 16)))
    up_saved = gaussian(key_list[7], (SLOTS, EXPERTS, FF), 1.0, 6.0, ((0, 16), (1, 16)))
    gate_weight = gaussian(key_list[8], (EXPERTS, D, FF), D ** -0.5, 0.09375, ((0, 16), (1, 16)))
    up_weight = gaussian(key_list[9], (EXPERTS, D, FF), D ** -0.5, 0.09375, ((0, 16), (1, 16)))
    down_weight = gaussian(key_list[10], (EXPERTS, FF, D), FF ** -0.5, 0.15625, ((0, 16), (2, 16)))
    return dict(attn_input=attn_input, query_grad=query_grad, query_weight=query_weight, moe_cotangent=moe_cotangent, expert_ids=expert_ids, route_weights=route_weights, gate_saved=gate_saved, up_saved=up_saved, gate_weight=gate_weight, up_weight=up_weight, down_weight=down_weight)


step_rate = 0.01
epsilon = 1e-06

def slot_tables(expert_ids, route_weights, experts, capacity):
    expert_iota = lax.broadcasted_iota(jnp.int32, (1, 1, experts), 2)
    chosen = (expert_ids[:, :, None] == expert_iota).astype(jnp.int32)
    counts = lax.optimization_barrier(jnp.sum(chosen, axis=1, dtype=jnp.int32))
    before = jnp.cumsum(counts, axis=0, dtype=jnp.int32) - counts
    position = lax.optimization_barrier(jnp.sum(chosen * before[:, None, :], axis=2, dtype=jnp.int32))
    slot_code = position * experts + expert_ids
    slot_iota = lax.broadcasted_iota(jnp.int32, (1, 1, capacity * experts), 2)
    matched = slot_code[:, :, None] == slot_iota
    select = lax.optimization_barrier(jnp.sum(matched.astype(route_weights.dtype), axis=1))
    scaled = lax.optimization_barrier(jnp.sum(jnp.where(matched, route_weights[:, :, None], 0.0), axis=1))
    return (select, scaled)

def activation_grads(hidden, gate_vals, up_vals):
    gate_float = gate_vals.astype(jnp.float32)
    up_float = up_vals.astype(jnp.float32)
    sigmoid_vals = jax.nn.sigmoid(gate_float)
    gate_grad = hidden * up_float * sigmoid_vals * (1.0 + gate_float * (1.0 - sigmoid_vals))
    up_grad = hidden * gate_float * sigmoid_vals
    return (gate_grad.astype(jnp.bfloat16), up_grad.astype(jnp.bfloat16))

def expert_backward(operands):
    slot_rows, gate_vals, up_vals, gate_w, up_w, down_w = operands
    width = slot_rows.shape[1]
    split_rows = slot_rows.reshape(SLOTS, N_DP, width // N_DP).astype(jnp.float32)
    split_down = down_w.reshape(FF, N_DP, width // N_DP).astype(jnp.float32)
    partial_sums = jnp.einsum('snc,hnc->nsh', split_rows, split_down)
    rounded = lax.optimization_barrier(partial_sums.astype(jnp.bfloat16))
    hidden = lax.optimization_barrier(jnp.sum(rounded.astype(jnp.float32), axis=0))
    gate_grad, up_grad = activation_grads(hidden, gate_vals, up_vals)
    total = jnp.dot(gate_grad, gate_w.T, preferred_element_type=jnp.float32)
    total = total + jnp.dot(up_grad, up_w.T, preferred_element_type=jnp.float32)
    return total.astype(jnp.bfloat16)

def reference(attn_input, query_grad, query_weight, moe_cotangent, expert_ids, route_weights, gate_saved, up_saved, gate_weight, up_weight, down_weight):
    batches = (attn_input.reshape(N_DP, TOK_ATT, D), query_grad.reshape(N_DP, TOK_ATT, QCOLS))

    def add_batch(total, pair):
        inputs, grads = pair
        term = lax.dot_general(grads, inputs, (((0,), (0,)), ((), ())), preferred_element_type=jnp.float32)
        rounded = lax.optimization_barrier(term.astype(jnp.bfloat16))
        return (total + rounded.astype(jnp.float32), None)
    gradient, unused = lax.scan(add_batch, jnp.zeros((QCOLS, D), jnp.float32), batches)
    radial = lax.optimization_barrier(jnp.mean(query_weight * gradient, axis=1, keepdims=True)) / (lax.optimization_barrier(jnp.mean(query_weight * query_weight, axis=1, keepdims=True)) + epsilon)
    stepped = query_weight - step_rate * (gradient - radial * query_weight)
    query_weight_next = stepped * lax.rsqrt(lax.optimization_barrier(jnp.mean(stepped * stepped, axis=1, keepdims=True)) + epsilon)
    block_ids = expert_ids.reshape(N_EXPERT, TOK_MOE, TOPK)
    block_weights = route_weights.reshape(N_EXPERT, TOK_MOE, TOPK)
    block_rows = moe_cotangent.reshape(N_EXPERT, TOK_MOE, D)

    def dispatch(operands):
        ids_block, weights_block, rows_block = operands
        select, scaled = slot_tables(ids_block, weights_block, EXPERTS, CAP)
        sent = jnp.dot(scaled.T, rows_block.astype(jnp.float32), precision=lax.Precision.HIGHEST, preferred_element_type=jnp.float32)
        return (sent.astype(jnp.bfloat16), select.astype(jnp.bfloat16))
    sent, selects = lax.map(dispatch, (block_ids, block_weights, block_rows))
    per_expert = jnp.transpose(sent.reshape(N_EXPERT, CAP, EXPERTS, D), (2, 0, 1, 3)).reshape(EXPERTS, SLOTS, D)
    slot_grads = lax.map(expert_backward, (per_expert, jnp.transpose(gate_saved, (1, 0, 2)), jnp.transpose(up_saved, (1, 0, 2)), gate_weight, up_weight, down_weight))
    by_source = jnp.transpose(slot_grads.reshape(EXPERTS, N_EXPERT, CAP, D), (1, 2, 0, 3)).reshape(N_EXPERT, CAP * EXPERTS, D)

    def combine(operands):
        select, flat_rows = operands
        return jnp.dot(select, flat_rows, preferred_element_type=jnp.float32)
    moe_input_grad = lax.map(combine, (selects, by_source)).reshape(N_EXPERT * TOK_MOE, D)
    return (query_weight_next, moe_input_grad)
```

```python
import jax
import jax.numpy as jnp
from jax import lax
from jax.sharding import PartitionSpec as P

step_rate = 0.01
epsilon = 1e-06


def slot_tables(expert_ids, route_weights, experts, capacity):
    expert_iota = lax.broadcasted_iota(jnp.int32, (1, 1, experts), 2)
    chosen = (expert_ids[:, :, None] == expert_iota).astype(jnp.int32)
    counts = jnp.sum(chosen, axis=1, dtype=jnp.int32)
    rows = counts.shape[0]
    earlier = lax.broadcasted_iota(jnp.int32, (rows, rows), 1) < lax.broadcasted_iota(
        jnp.int32, (rows, rows), 0
    )
    before = jnp.dot(
        earlier.astype(jnp.bfloat16),
        counts.astype(jnp.bfloat16),
        preferred_element_type=jnp.float32,
    ).astype(jnp.int32)
    position = jnp.sum(chosen * before[:, None, :], axis=2, dtype=jnp.int32)
    slot_code = position * experts + expert_ids
    slot_iota = lax.broadcasted_iota(jnp.int32, (1, 1, capacity * experts), 2)
    matched = slot_code[:, :, None] == slot_iota
    select = jnp.sum(matched.astype(jnp.float32), axis=1)
    scaled = jnp.sum(jnp.where(matched, route_weights[:, :, None], 0.0), axis=1)
    return (select, scaled)


def activation_grads(hidden, gate_vals, up_vals):
    gate_float = gate_vals.astype(jnp.float32)
    up_float = up_vals.astype(jnp.float32)
    sigmoid_vals = jax.nn.sigmoid(gate_float)
    gate_grad = hidden * up_float * sigmoid_vals * (1.0 + gate_float * (1.0 - sigmoid_vals))
    up_grad = hidden * gate_float * sigmoid_vals
    return jnp.stack([gate_grad, up_grad], axis=2).astype(jnp.bfloat16)


def weight_update(attn_input, query_grad, query_weight):
    gradient = lax.psum_scatter(
        lax.dot_general(
            query_grad, attn_input, (((0,), (0,)), ((), ())), preferred_element_type=jnp.float32
        ).astype(jnp.bfloat16),
        "dp",
        scatter_dimension=0,
        tiled=True,
    ).astype(jnp.float32)
    radial = jnp.mean(query_weight * gradient, axis=1, keepdims=True) / (
        jnp.mean(query_weight * query_weight, axis=1, keepdims=True) + epsilon
    )
    stepped = query_weight - step_rate * (gradient - radial * query_weight)
    return stepped * lax.rsqrt(jnp.mean(stepped * stepped, axis=1, keepdims=True) + epsilon)


def expert_update(
    moe_cotangent,
    expert_ids,
    route_weights,
    gate_saved,
    up_saved,
    gate_weight,
    up_weight,
    down_weight,
):
    groups = lax.axis_size("expert")
    experts = gate_weight.shape[0] * groups
    capacity = gate_saved.shape[0] * lax.axis_size("dp") // groups
    select, scaled = slot_tables(expert_ids, route_weights, experts, capacity)
    outgoing = jnp.dot(
        scaled.T,
        moe_cotangent.astype(jnp.float32),
        precision=lax.Precision.HIGHEST,
        preferred_element_type=jnp.float32,
    )
    outgoing = outgoing.astype(jnp.bfloat16).reshape(capacity, experts, moe_cotangent.shape[1])
    arrived = lax.all_to_all(outgoing, "expert", split_axis=1, concat_axis=0, tiled=True)
    hidden = lax.psum_scatter(
        jnp.einsum("sec,ehc->seh", arrived, down_weight, preferred_element_type=jnp.float32).astype(
            jnp.bfloat16
        ),
        "dp",
        scatter_dimension=0,
        tiled=True,
    ).astype(jnp.float32)
    grads_pair = activation_grads(hidden, gate_saved, up_saved)
    part_rows = lax.all_gather(grads_pair, "dp", axis=0, tiled=True)
    total = jnp.einsum(
        "seh,ech->sec", part_rows[:, :, 0], gate_weight, preferred_element_type=jnp.float32
    )
    total = total + jnp.einsum(
        "seh,ech->sec", part_rows[:, :, 1], up_weight, preferred_element_type=jnp.float32
    )
    slot_input = total.astype(jnp.bfloat16)
    returned_rows = lax.all_to_all(slot_input, "expert", split_axis=0, concat_axis=1, tiled=True)
    flat_rows = returned_rows.reshape(capacity * experts, returned_rows.shape[2])
    return jnp.dot(select.astype(jnp.bfloat16), flat_rows, preferred_element_type=jnp.float32)


def shards(
    attn_input,
    query_grad,
    query_weight,
    moe_cotangent,
    expert_ids,
    route_weights,
    gate_saved,
    up_saved,
    gate_weight,
    up_weight,
    down_weight,
):
    moe_input_grad = expert_update(
        moe_cotangent,
        expert_ids,
        route_weights,
        gate_saved,
        up_saved,
        gate_weight,
        up_weight,
        down_weight,
    )
    query_weight_next = weight_update(attn_input, query_grad, query_weight)
    return (query_weight_next, moe_input_grad)


def solution(mesh):
    placed = (
        P("dp", None),
        P("dp", "expert"),
        P(("expert", "dp"), None),
        P("expert", "dp"),
        P("expert", None),
        P("expert", None),
        P("dp", "expert", None),
        P("dp", "expert", None),
        P("expert", "dp", None),
        P("expert", "dp", None),
        P("expert", None, "dp"),
    )
    return jax.shard_map(
        shards,
        mesh=mesh,
        in_specs=placed,
        out_specs=(P(("expert", "dp"), None), P("expert", "dp")),
        check_vma=False,
    )
```

```python
import functools

import jax
import jax.numpy as jnp
from jax import lax
from jax.experimental import pallas as pl
from jax.experimental.pallas import tpu as pltpu
from jax.sharding import PartitionSpec as P

STEP_RATE = 0.01
EPSILON = 1e-06
MESH = pl.DeviceIdType.MESH
NZ = 8
NE = 16
LANES = 4
NT = (((1,), (1,)), ((), ()))
BF = jnp.bfloat16
F32 = jnp.float32


def remote(src, dst, send_sem, recv_sem, device):
    return pltpu.make_async_remote_copy(
        src_ref=src,
        dst_ref=dst,
        send_sem=send_sem,
        recv_sem=recv_sem,
        device_id=device,
        device_id_type=MESH,
    )


def sign(lane):
    return 1 if lane < 2 else -1


def step_kernel(
    ids_ref,
    route_ref,
    cot_ref,
    grad_hbm,
    input_hbm,
    weight_hbm,
    gate_hbm,
    up_hbm,
    gate_w_hbm,
    up_w_hbm,
    down_w_hbm,
    query_out,
    moe_out,
    grad_v,
    grad_t,
    input_v,
    weight_v,
    gate_v,
    up_v,
    gate_w,
    up_w,
    down_w,
    onehot,
    outgoing,
    arrived,
    q_part,
    q_recv,
    q_give,
    q_take,
    h_part,
    h_recv,
    h_give,
    h_take,
    grads,
    result,
    returned,
    load_sem,
    disp_send,
    disp_recv,
    q_send,
    q_got,
    qx_send,
    qx_got,
    h_send,
    h_got,
    hx_send,
    hx_got,
    g_send,
    g_got,
    gx_send,
    gx_got,
    r_send,
    r_got,
):
    e = lax.axis_index("expert")
    d = lax.axis_index("dp")
    h = d // NZ
    z = lax.rem(d, NZ)
    twin = (e, (1 - h) * NZ + z)
    ahead = (e, h * NZ + lax.rem(z + 1, NZ))
    behind = (e, h * NZ + lax.rem(z + NZ - 1, NZ))

    def toward(lane):
        return ahead if sign(lane) > 0 else behind

    def at_z(lane, hops):
        return lax.rem(z + 4 * NZ - sign(lane) * hops, NZ)

    loads = [
        pltpu.make_async_copy(src, dst, load_sem.at[i])
        for i, (src, dst) in enumerate(
            (
                (grad_hbm, grad_v),
                (input_hbm, input_v),
                (down_w_hbm, down_w),
                (gate_hbm, gate_v),
                (up_hbm, up_v),
                (gate_w_hbm, gate_w),
                (up_w_hbm, up_w),
                (weight_hbm, weight_v),
            )
        )
    ]
    for copy in loads:
        copy.start()

    barrier = pltpu.get_barrier_semaphore()

    @pl.loop(1, NE)
    def _(k):
        pl.semaphore_signal(
            barrier, inc=1, device_id=(lax.rem(e + k, NE), d), device_id_type=MESH
        )

    for device in (ahead, behind, twin):
        pl.semaphore_signal(barrier, inc=1, device_id=device, device_id_type=MESH)

    experts = 2 * NE
    tokens = ids_ref.shape[1]
    slots = outgoing.shape[1]
    which = lax.broadcasted_iota(jnp.int32, (experts, tokens), 0)
    chosen = jnp.zeros((experts, tokens), F32)
    share = jnp.zeros((experts, tokens), F32)
    for k in range(ids_ref.shape[0]):
        hit = ids_ref[k : k + 1, :] == which
        chosen = chosen + jnp.where(hit, 1.0, 0.0)
        share = share + jnp.where(hit, route_ref[k : k + 1, :], 0.0)
    earlier = lax.broadcasted_iota(jnp.int32, (tokens, tokens), 0) < lax.broadcasted_iota(
        jnp.int32, (tokens, tokens), 1
    )
    before = jnp.dot(
        chosen.astype(BF), jnp.where(earlier, 1.0, 0.0).astype(BF), preferred_element_type=F32
    )
    position = jnp.where(chosen > 0.5, before, -1.0).astype(jnp.int32)
    slot_iota = lax.broadcasted_iota(jnp.int32, (slots, tokens), 0)
    cot = cot_ref[...]
    for block in range(experts):
        mine = position[block : block + 1, :] == slot_iota
        scale = jnp.sum(
            jnp.where(mine, share[block : block + 1, :], 0.0), axis=1, keepdims=True
        )
        pick = jnp.where(mine, 1.0, 0.0).astype(BF)
        onehot[block] = pick
        rows = jnp.dot(pick, cot, preferred_element_type=F32)
        outgoing[block] = (rows * scale).astype(BF)

    pl.semaphore_wait(barrier, NE + 2)

    def dispatch(k):
        to = lax.rem(e + k, NE)
        return remote(
            outgoing.at[pl.ds(2 * to, 2)],
            arrived.at[:, e],
            disp_send.at[k],
            disp_recv.at[k],
            (to, d),
        )

    @pl.loop(1, NE)
    def _(k):
        dispatch(k).start()

    arrived[:, e] = outgoing[pl.ds(2 * e, 2)]

    def ring(part, recv, send, got, lane, t):
        src = part.at[lane, :, at_z(lane, 1)] if isinstance(t, int) else recv.at[lane, t - 1]
        return remote(src, recv.at[lane, t], send.at[lane, t], got.at[lane, t], toward(lane))

    def await_step(recv, send, got, lane, t):
        at = recv.at[lane, t]
        remote(at, at, send.at[lane, t], got.at[lane, t], toward(lane)).wait_recv()

    def forward(part, recv, send, got, lane, t):
        await_step(recv, send, got, lane, t - 1)
        total = recv[lane, t - 1].astype(F32) + part[lane, :, at_z(lane, 1 + t)].astype(F32)
        recv[lane, t - 1] = total.astype(BF)
        ring(part, recv, send, got, lane, t).start()

    loads[0].wait()
    loads[1].wait()
    grad_t[...] = grad_v[...].T
    q_wide = q_part.shape[-1]
    for lane in range(LANES):

        @pl.loop(0, q_wide // 256)
        def _(j):
            columns = pl.ds(pl.multiple_of(lane * q_wide + j * 256, 256), 256)
            part = jnp.dot(grad_t[...], input_v[:, columns], preferred_element_type=F32)
            q_part[lane, :, :, :, pl.ds(pl.multiple_of(j * 256, 256), 256)] = part.astype(
                BF
            ).reshape(2, NZ, 32, 256)

        ring(q_part, q_recv, q_send, q_got, lane, 0).start()

    @pl.loop(1, NE)
    def _(k):
        dispatch(k).wait_recv()

    loads[2].wait()
    h_wide = h_part.shape[-1]
    for lane in range(LANES):
        expert, half = lane // 2, lane % 2

        @pl.loop(0, h_wide // 256)
        def _(j):
            rows = pl.ds(pl.multiple_of(half * h_wide + j * 256, 256), 256)
            part = lax.dot_general(
                arrived[expert].reshape(NE * slots, -1),
                down_w[expert, rows, :],
                NT,
                preferred_element_type=F32,
            )
            h_part[lane, :, :, :, pl.ds(pl.multiple_of(j * 256, 256), 256)] = part.astype(
                BF
            ).reshape(2, NZ, slots, 256)

        ring(h_part, h_recv, h_send, h_got, lane, 0).start()

    @pl.loop(1, NZ - 1)
    def _(t):
        for lane in range(LANES):
            forward(q_part, q_recv, q_send, q_got, lane, t)
        for lane in range(LANES):
            forward(h_part, h_recv, h_send, h_got, lane, t)

    last = NZ - 2

    def exchange(give, take, send, got, lane):
        return remote(give.at[lane], take.at[lane], send.at[lane], got.at[lane], twin)

    def settle(part, recv, send, got, give, take, x_send, x_got, lane):
        await_step(recv, send, got, lane, last)
        theirs = recv[lane, last, 1 - h].astype(F32) + part[lane, 1 - h, z].astype(F32)
        give[lane] = theirs.astype(BF)
        exchange(give, take, x_send, x_got, lane).start()

    def total_of(part, recv, give, take, x_send, x_got, lane):
        exchange(give, take, x_send, x_got, lane).wait_recv()
        mine = recv[lane, last, h].astype(F32) + part[lane, h, z].astype(F32)
        return mine + take[lane].astype(F32)

    for lane in range(LANES):
        settle(h_part, h_recv, h_send, h_got, h_give, h_take, hx_send, hx_got, lane)
    for i in (3, 4, 5, 6, 7):
        loads[i].wait()

    def gather(lane, chain, t):
        side = h if chain == 0 else 1 - h
        at = grads.at[lane, side, at_z(lane, t)]
        return remote(at, at, g_send.at[lane, chain, t], g_got.at[lane, chain, t], toward(lane))

    def swap(lane):
        at = grads.at[lane, h, z]
        return remote(at, at, gx_send.at[lane], gx_got.at[lane], twin)

    for expert in range(2):
        for half in range(2):
            lane = 2 * expert + half
            hidden = total_of(h_part, h_recv, h_give, h_take, hx_send, hx_got, lane)
            columns = slice(half * h_wide, (half + 1) * h_wide)
            g = gate_v[:, expert, columns].astype(F32)
            u = up_v[:, expert, columns].astype(F32)
            sigma = 1.0 / (1.0 + jnp.exp(-g))
            grads[2 * expert, h, z, :, columns] = (
                hidden * u * sigma * (1.0 + g * (1.0 - sigma))
            ).astype(BF)
            grads[2 * expert + 1, h, z, :, columns] = (hidden * g * sigma).astype(BF)
        for lane in (2 * expert, 2 * expert + 1):
            gather(lane, 0, 0).start()
            swap(lane).start()

    for lane in range(LANES):
        remote_in = swap(lane)
        remote_in.wait_recv()
        gather(lane, 1, 0).start()
    for lane in range(LANES):
        settle(q_part, q_recv, q_send, q_got, q_give, q_take, qx_send, qx_got, lane)

    def reply(expert, side, block):
        to = side * NZ + block
        return remote(
            result.at[expert, side, block],
            returned.at[e, expert],
            r_send.at[expert, side, block],
            r_got.at[e, expert],
            (to, d),
        )

    def produce(expert, block):
        gate = grads[2 * expert, :, block].reshape(2 * slots, -1)
        up = grads[2 * expert + 1, :, block].reshape(2 * slots, -1)
        rows = lax.dot_general(gate, gate_w[expert], NT, preferred_element_type=F32)
        rows = rows + lax.dot_general(up, up_w[expert], NT, preferred_element_type=F32)
        rows = rows.astype(BF).reshape(2, slots, -1)
        for side in range(2):
            result[expert, side, block] = rows[side]
            to = side * NZ + block

            @pl.when(to == e)
            def _():
                returned[e, expert] = rows[side]

            @pl.when(to != e)
            def _():
                reply(expert, side, block).start()

    for expert in range(2):
        produce(expert, z)

    @pl.loop(0, NZ - 1)
    def _(t):
        for lane in range(LANES):
            for chain in range(2):
                gather(lane, chain, t).wait_recv()

                @pl.when(t < NZ - 2)
                def _():
                    gather(lane, chain, t + 1).start()

        for expert in range(2):
            produce(expert, at_z(2 * expert, t + 1))

    for lane in range(LANES):
        columns = slice(lane * q_wide, (lane + 1) * q_wide)
        query_out[:, columns] = total_of(
            q_part, q_recv, q_give, q_take, qx_send, qx_got, lane
        )
    gradient = query_out[...]
    weight = weight_v[...]
    count = 1.0 / weight.shape[1]
    radial = (jnp.sum(weight * gradient, axis=1, keepdims=True) * count) / (
        jnp.sum(weight * weight, axis=1, keepdims=True) * count + EPSILON
    )
    stepped = weight - STEP_RATE * (gradient - radial * weight)
    norm = jnp.sum(stepped * stepped, axis=1, keepdims=True) * count + EPSILON
    query_out[...] = stepped * lax.rsqrt(norm)

    @pl.loop(1, NE)
    def _(k):
        source = lax.rem(e + k, NE)
        for expert in range(2):
            at = returned.at[source, expert]
            remote(
                at, at, r_send.at[expert, 0, 0], r_got.at[source, expert], twin
            ).wait_recv()

    moe_out[...] = lax.dot_general(
        onehot[...].reshape(experts * slots, tokens),
        returned[...].reshape(experts * slots, -1),
        (((0,), (0,)), ((), ())),
        preferred_element_type=F32,
    )

    @pl.loop(1, NE)
    def _(k):
        dispatch(k).wait_send()

    for lane in range(LANES):
        ring(q_part, q_recv, q_send, q_got, lane, 0).wait_send()
        ring(h_part, h_recv, h_send, h_got, lane, 0).wait_send()
        exchange(q_give, q_take, qx_send, qx_got, lane).wait_send()
        exchange(h_give, h_take, hx_send, hx_got, lane).wait_send()
        swap(lane).wait_send()

    @pl.loop(1, NZ - 1)
    def _(t):
        for lane in range(LANES):
            ring(q_part, q_recv, q_send, q_got, lane, t).wait_send()
            ring(h_part, h_recv, h_send, h_got, lane, t).wait_send()

    @pl.loop(0, NZ - 1)
    def _(t):
        for lane in range(LANES):
            for chain in range(2):
                gather(lane, chain, t).wait_send()

    @pl.loop(0, NZ)
    def _(block):
        for side in range(2):

            @pl.when(side * NZ + block != e)
            def _():
                for expert in range(2):
                    reply(expert, side, block).wait_send()


def shards(
    attn_input,
    query_grad,
    query_weight,
    moe_cotangent,
    expert_ids,
    route_weights,
    gate_saved,
    up_saved,
    gate_weight,
    up_weight,
    down_weight,
):
    vmem = pl.BlockSpec(memory_space=pltpu.VMEM)
    hbm = pl.BlockSpec(memory_space=pl.ANY)
    dma = pltpu.SemaphoreType.DMA
    tokens, width = moe_cotangent.shape
    slots, local, hidden = gate_saved.shape
    rows, model = query_weight.shape
    batch, heads = query_grad.shape
    q_wide, h_wide = model // LANES, local * hidden // LANES
    scratch = [
        pltpu.VMEM(query_grad.shape, BF),
        pltpu.VMEM((heads, batch), BF),
        pltpu.VMEM(attn_input.shape, BF),
        pltpu.VMEM(query_weight.shape, F32),
        pltpu.VMEM(gate_saved.shape, BF),
        pltpu.VMEM(up_saved.shape, BF),
        pltpu.VMEM(gate_weight.shape, BF),
        pltpu.VMEM(up_weight.shape, BF),
        pltpu.VMEM(down_weight.shape, BF),
        pltpu.VMEM((local * NE, slots, tokens), BF),
        pltpu.VMEM((local * NE, slots, width), BF),
        pltpu.VMEM((local, NE, slots, width), BF),
        pltpu.VMEM((LANES, 2, NZ, rows, q_wide), BF),
        pltpu.VMEM((LANES, NZ - 1, 2, rows, q_wide), BF),
        pltpu.VMEM((LANES, rows, q_wide), BF),
        pltpu.VMEM((LANES, rows, q_wide), BF),
        pltpu.VMEM((LANES, 2, NZ, slots, h_wide), BF),
        pltpu.VMEM((LANES, NZ - 1, 2, slots, h_wide), BF),
        pltpu.VMEM((LANES, slots, h_wide), BF),
        pltpu.VMEM((LANES, slots, h_wide), BF),
        pltpu.VMEM((LANES, 2, NZ, slots, hidden), BF),
        pltpu.VMEM((local, 2, NZ, slots, width), BF),
        pltpu.VMEM((NE, local, slots, width), BF),
        dma((8,)),
        dma((NE,)),
        dma((NE,)),
        dma((LANES, NZ - 1)),
        dma((LANES, NZ - 1)),
        dma((LANES,)),
        dma((LANES,)),
        dma((LANES, NZ - 1)),
        dma((LANES, NZ - 1)),
        dma((LANES,)),
        dma((LANES,)),
        dma((LANES, 2, NZ - 1)),
        dma((LANES, 2, NZ - 1)),
        dma((LANES,)),
        dma((LANES,)),
        dma((local, 2, NZ)),
        dma((NE, local)),
    ]
    return pl.pallas_call(
        step_kernel,
        name="backward_step",
        out_shape=(
            jax.ShapeDtypeStruct((rows, model), F32),
            jax.ShapeDtypeStruct((tokens, width), F32),
        ),
        in_specs=[vmem, vmem, vmem] + [hbm] * 8,
        out_specs=(vmem, vmem),
        scratch_shapes=scratch,
        compiler_params=pltpu.CompilerParams(
            collective_id=0, has_side_effects=True, vmem_limit_bytes=58 << 20
        ),
    )(
        expert_ids.T,
        route_weights.T,
        moe_cotangent,
        query_grad,
        attn_input,
        query_weight,
        gate_saved,
        up_saved,
        gate_weight,
        up_weight,
        down_weight,
    )


def solution(mesh):
    placed = (
        P("dp", None),
        P("dp", "expert"),
        P(("expert", "dp"), None),
        P("expert", "dp"),
        P("expert", None),
        P("expert", None),
        P("dp", "expert", None),
        P("dp", "expert", None),
        P("expert", "dp", None),
        P("expert", "dp", None),
        P("expert", None, "dp"),
    )
    return jax.shard_map(
        shards,
        mesh=mesh,
        in_specs=placed,
        out_specs=(P(("expert", "dp"), None), P("expert", "dp")),
        check_vma=False,
    )
```

```python
import functools

import jax
import jax.numpy as jnp
from jax import lax
from jax.experimental import pallas as pl
from jax.experimental.pallas import tpu as pltpu
from jax.sharding import PartitionSpec as P

STEP_RATE = 0.01
EPSILON = 1e-06
MESH = pl.DeviceIdType.MESH
NZ = 8
NE = 16
LANES = 4
NT = (((1,), (1,)), ((), ()))
BF = jnp.bfloat16
F32 = jnp.float32


def remote(src, dst, send_sem, recv_sem, device):
    return pltpu.make_async_remote_copy(
        src_ref=src,
        dst_ref=dst,
        send_sem=send_sem,
        recv_sem=recv_sem,
        device_id=device,
        device_id_type=MESH,
    )


def sign(lane):
    return 1 if lane < 2 else -1


def step_kernel(
    ids_ref,
    route_ref,
    cot_ref,
    grad_hbm,
    input_hbm,
    weight_hbm,
    gate_hbm,
    up_hbm,
    gate_w_hbm,
    up_w_hbm,
    down_w_hbm,
    query_out,
    moe_out,
    grad_v,
    grad_t,
    input_v,
    weight_v,
    gate_v,
    up_v,
    gate_w,
    up_w,
    down_w,
    cot_in,
    onehot,
    scale,
    outgoing,
    arrived,
    q_part,
    q_recv,
    q_give,
    q_take,
    h_part,
    h_recv,
    grads,
    result,
    returned,
    load_sem,
    disp_send,
    disp_recv,
    pair_send,
    pair_got,
    q_send,
    q_got,
    qx_send,
    qx_got,
    h_send,
    h_got,
    g_send,
    g_got,
    r_send,
    r_got,
):
    e = lax.axis_index("expert")
    d = lax.axis_index("dp")
    h = d // NZ
    z = lax.rem(d, NZ)
    twin_d = (1 - h) * NZ + z
    twin = (e, twin_d)
    ahead = (e, h * NZ + lax.rem(z + 1, NZ))
    behind = (e, h * NZ + lax.rem(z + NZ - 1, NZ))
    units = gate_w.shape[-1]
    slots = gate_v.shape[1]
    experts = 2 * NE
    tokens = ids_ref.shape[1]

    def toward(lane):
        return ahead if sign(lane) > 0 else behind

    def at_z(lane, hops):
        return lax.rem(z + 4 * NZ - sign(lane) * hops, NZ)

    own = pl.ds(pl.multiple_of(h * units, 128), units)
    other = pl.ds(pl.multiple_of((1 - h) * units, 128), units)
    loads = [
        pltpu.make_async_copy(src, dst, load_sem.at[i])
        for i, (src, dst) in enumerate(
            (
                (grad_hbm, grad_v),
                (input_hbm, input_v),
                (down_w_hbm.at[:, h], down_w.at[h]),
                (gate_hbm.at[:, :, own], gate_v.at[h]),
                (up_hbm.at[:, :, own], up_v.at[h]),
                (gate_w_hbm.at[:, :, own], gate_w.at[h]),
                (up_w_hbm.at[:, :, own], up_w.at[h]),
                (weight_hbm, weight_v),
            )
        )
    ]
    shares = [
        remote(src, dst, pair_send.at[i], pair_got.at[i], twin)
        for i, (src, dst) in enumerate(
            (
                (cot_ref, cot_in),
                (down_w_hbm.at[:, 1 - h], down_w.at[h]),
                (gate_hbm.at[:, :, other], gate_v.at[h]),
                (up_hbm.at[:, :, other], up_v.at[h]),
                (gate_w_hbm.at[:, :, other], gate_w.at[h]),
                (up_w_hbm.at[:, :, other], up_w.at[h]),
            )
        )
    ]
    for copy in loads:
        copy.start()

    barrier = pltpu.get_barrier_semaphore()

    for device in (twin, ahead, behind):
        pl.semaphore_signal(barrier, inc=1, device_id=device, device_id_type=MESH)

    @pl.loop(1, NE)
    def _(k):
        for column in (d, twin_d):
            pl.semaphore_signal(
                barrier, inc=1, device_id=(lax.rem(e + k, NE), column), device_id_type=MESH
            )

    which = lax.broadcasted_iota(jnp.int32, (experts, tokens), 0)
    chosen = jnp.zeros((experts, tokens), F32)
    share = jnp.zeros((experts, tokens), F32)
    for k in range(ids_ref.shape[0]):
        hit = ids_ref[k : k + 1, :] == which
        chosen = chosen + jnp.where(hit, 1.0, 0.0)
        share = share + jnp.where(hit, route_ref[k : k + 1, :], 0.0)
    earlier = lax.broadcasted_iota(jnp.int32, (tokens, tokens), 0) < lax.broadcasted_iota(
        jnp.int32, (tokens, tokens), 1
    )
    before = jnp.dot(
        chosen.astype(BF), jnp.where(earlier, 1.0, 0.0).astype(BF), preferred_element_type=F32
    )
    position = jnp.where(chosen > 0.5, before, -1.0).astype(jnp.int32)
    slot_iota = lax.broadcasted_iota(jnp.int32, (slots, tokens), 0)
    for block in range(experts):
        mine = position[block : block + 1, :] == slot_iota
        scale[block] = jnp.sum(
            jnp.where(mine, share[block : block + 1, :], 0.0), axis=1, keepdims=True
        )
        onehot[block] = jnp.where(mine, 1.0, 0.0).astype(BF)

    def fill(side, cot):
        group = 8
        for first in range(0, experts, group):
            picks = onehot[first : first + group].reshape(group * slots, tokens)
            rows = jnp.dot(picks, cot, preferred_element_type=F32)
            rows = rows * scale[first : first + group].reshape(group * slots, 1)
            outgoing[side, first : first + group] = rows.astype(BF).reshape(group, slots, -1)

    fill(h, cot_ref[...])

    pl.semaphore_wait(barrier, 2 * NE + 1)
    shares[0].start()
    shares[1].start()

    def dispatch(side, k):
        to = lax.rem(e + k, NE)
        return remote(
            outgoing.at[side, pl.ds(2 * to, 2)],
            arrived.at[side, :, e],
            disp_send.at[side, k],
            disp_recv.at[side, k],
            (to, d),
        )

    def dispatch_all(side):
        @pl.loop(1, NE)
        def _(k):
            dispatch(side, k).start()

        arrived[side, :, e] = outgoing[side, pl.ds(2 * e, 2)]

    dispatch_all(h)
    shares[0].wait_recv()
    fill(1 - h, cot_in[...])
    dispatch_all(1 - h)

    def ring(part, recv, send, got, lane, t):
        src = part.at[lane, :, at_z(lane, 1)] if isinstance(t, int) else recv.at[lane, t - 1]
        return remote(src, recv.at[lane, t], send.at[lane, t], got.at[lane, t], toward(lane))

    def await_step(recv, send, got, lane, t):
        at = recv.at[lane, t]
        remote(at, at, send.at[lane, t], got.at[lane, t], toward(lane)).wait_recv()

    def forward(part, recv, send, got, t):
        for lane in range(LANES):
            await_step(recv, send, got, lane, t - 1)
            total = recv[lane, t - 1].astype(F32) + part[lane, :, at_z(lane, 1 + t)].astype(F32)
            recv[lane, t - 1] = total.astype(BF)
            ring(part, recv, send, got, lane, t).start()

    def q_forward(t):
        forward(q_part, q_recv, q_send, q_got, t)

    def h_forward(t):
        forward(h_part, h_recv, h_send, h_got, t)

    loads[0].wait()
    loads[1].wait()
    grad_t[...] = grad_v[...].T
    q_wide = q_part.shape[-1]
    for lane in range(LANES):

        @pl.loop(0, q_wide // 256)
        def _(j):
            columns = pl.ds(pl.multiple_of(lane * q_wide + j * 256, 256), 256)
            part = jnp.dot(grad_t[...], input_v[:, columns], preferred_element_type=F32)
            q_part[lane, :, :, :, pl.ds(pl.multiple_of(j * 256, 256), 256)] = part.astype(
                BF
            ).reshape(2, NZ, 32, 256)

        ring(q_part, q_recv, q_send, q_got, lane, 0).start()

    @pl.loop(1, 3)
    def _(t):
        q_forward(t)

    @pl.loop(1, NE)
    def _(k):
        for side in range(2):
            dispatch(side, k).wait_recv()

    loads[2].wait()
    shares[1].wait_recv()
    for copy in shares[2:]:
        copy.start()
    h_wide = h_part.shape[-1]
    for lane in range(LANES):
        expert, half = lane // 2, lane % 2
        rows = slice(half * h_wide, (half + 1) * h_wide)

        @pl.loop(0, 2)
        def _(block_side):
            part = 0.0
            for side in range(2):
                part = part + lax.dot_general(
                    arrived[side, expert, pl.ds(block_side * NZ, NZ)].reshape(NZ * slots, -1),
                    down_w[side, expert, rows, :],
                    NT,
                    preferred_element_type=F32,
                )
            h_part[lane, block_side] = part.astype(BF).reshape(NZ, slots, h_wide)

        ring(h_part, h_recv, h_send, h_got, lane, 0).start()

    @pl.loop(0, 3)
    def _(p):
        h_forward(2 * p + 1)
        h_forward(2 * p + 2)
        q_forward(p + 3)

    q_forward(jnp.int32(NZ - 2))
    last = NZ - 2

    def gather(lane, t):
        at = grads.at[lane, :, at_z(lane, t)]
        return remote(at, at, g_send.at[lane, t], g_got.at[lane, t], toward(lane))

    for i in (3, 4, 5, 6, 7):
        loads[i].wait()
    for i in (2, 3):
        shares[i].wait_recv()
    for expert in range(2):
        for half in range(2):
            lane = 2 * expert + half
            await_step(h_recv, h_send, h_got, lane, last)
            columns = slice(half * h_wide, (half + 1) * h_wide)
            for side in range(2):
                hidden = h_recv[lane, last, side].astype(F32) + h_part[lane, side, z].astype(F32)
                g = gate_v[side, :, expert, columns].astype(F32)
                u = up_v[side, :, expert, columns].astype(F32)
                sigma = 1.0 / (1.0 + jnp.exp(-g))
                grads[2 * expert, side, z, :, columns] = (
                    hidden * u * sigma * (1.0 + g * (1.0 - sigma))
                ).astype(BF)
                grads[2 * expert + 1, side, z, :, columns] = (hidden * g * sigma).astype(BF)
        for lane in (2 * expert, 2 * expert + 1):
            gather(lane, 0).start()

    def exchange(lane):
        return remote(q_give.at[lane], q_take.at[lane], qx_send.at[lane], qx_got.at[lane], twin)

    for lane in range(LANES):
        await_step(q_recv, q_send, q_got, lane, last)
        theirs = q_recv[lane, last, 1 - h].astype(F32) + q_part[lane, 1 - h, z].astype(F32)
        q_give[lane] = theirs.astype(BF)
        exchange(lane).start()

    def reply(expert, width, side, block):
        at = result.at[expert, width, side, block]
        return remote(
            at,
            returned.at[h, e, expert],
            r_send.at[expert, width, side, block],
            r_got.at[h, e, expert],
            (side * NZ + block, width * NZ + z),
        )

    def produce(expert, block):
        gate = grads[2 * expert, :, block].reshape(2 * slots, -1)
        up = grads[2 * expert + 1, :, block].reshape(2 * slots, -1)
        for width in range(2):
            rows = lax.dot_general(gate, gate_w[width, expert], NT, preferred_element_type=F32)
            rows = rows + lax.dot_general(
                up, up_w[width, expert], NT, preferred_element_type=F32
            )
            rows = rows.astype(BF).reshape(2, slots, -1)
            for side in range(2):
                result[expert, width, side, block] = rows[side]
                here = (side * NZ + block == e) & (width == h)

                @pl.when(here)
                def _():
                    returned[h, e, expert] = rows[side]

                @pl.when(jnp.logical_not(here))
                def _():
                    reply(expert, width, side, block).start()

    for i in (4, 5):
        shares[i].wait_recv()
    for expert in range(2):
        produce(expert, z)

    @pl.loop(0, NZ - 2)
    def _(t):
        for lane in range(LANES):
            gather(lane, t).wait_recv()
            gather(lane, t + 1).start()

        for expert in range(2):
            produce(expert, at_z(2 * expert, t + 1))

    for lane in range(LANES):
        exchange(lane).wait_recv()
        mine = q_recv[lane, last, h].astype(F32) + q_part[lane, h, z].astype(F32)
        query_out[:, lane * q_wide : (lane + 1) * q_wide] = mine + q_take[lane].astype(F32)
    gradient = query_out[...]
    weight = weight_v[...]
    count = 1.0 / weight.shape[1]
    radial = (jnp.sum(weight * gradient, axis=1, keepdims=True) * count) / (
        jnp.sum(weight * weight, axis=1, keepdims=True) * count + EPSILON
    )
    stepped = weight - STEP_RATE * (gradient - radial * weight)
    norm = jnp.sum(stepped * stepped, axis=1, keepdims=True) * count + EPSILON
    query_out[...] = stepped * lax.rsqrt(norm)

    for expert in range(2):
        for lane in (2 * expert, 2 * expert + 1):
            gather(lane, NZ - 2).wait_recv()
        produce(expert, at_z(2 * expert, NZ - 1))

    @pl.loop(0, NE)
    def _(source):
        for half in range(2):

            @pl.when(jnp.logical_not((source == e) & (half == h)))
            def _():
                for expert in range(2):
                    at = returned.at[half, source, expert]
                    remote(
                        at, at, r_send.at[expert, 0, 0, 0], r_got.at[half, source, expert], twin
                    ).wait_recv()

    total = 0.0
    for half in range(2):
        total = total + lax.dot_general(
            onehot[...].reshape(experts * slots, tokens),
            returned[half].reshape(experts * slots, -1),
            (((0,), (0,)), ((), ())),
            preferred_element_type=F32,
        )
    moe_out[...] = total

    for copy in shares:
        copy.wait_send()

    @pl.loop(1, NE)
    def _(k):
        for side in range(2):
            dispatch(side, k).wait_send()

    for lane in range(LANES):
        ring(q_part, q_recv, q_send, q_got, lane, 0).wait_send()
        ring(h_part, h_recv, h_send, h_got, lane, 0).wait_send()
        exchange(lane).wait_send()

    @pl.loop(1, NZ - 1)
    def _(t):
        for lane in range(LANES):
            ring(q_part, q_recv, q_send, q_got, lane, t).wait_send()
            ring(h_part, h_recv, h_send, h_got, lane, t).wait_send()

    @pl.loop(0, NZ - 1)
    def _(t):
        for lane in range(LANES):
            gather(lane, t).wait_send()

    @pl.loop(0, NZ)
    def _(block):
        for side in range(2):
            for width in range(2):

                @pl.when(jnp.logical_not((side * NZ + block == e) & (width == h)))
                def _():
                    for expert in range(2):
                        reply(expert, width, side, block).wait_send()


def shards(
    attn_input,
    query_grad,
    query_weight,
    moe_cotangent,
    expert_ids,
    route_weights,
    gate_saved,
    up_saved,
    gate_weight,
    up_weight,
    down_weight,
):
    vmem = pl.BlockSpec(memory_space=pltpu.VMEM)
    hbm = pl.BlockSpec(memory_space=pl.ANY)
    dma = pltpu.SemaphoreType.DMA
    tokens, width = moe_cotangent.shape
    slots, local, hidden = gate_saved.shape
    rows, model = query_weight.shape
    batch, heads = query_grad.shape
    units = hidden // 2
    q_wide, h_wide = model // LANES, local * units // LANES
    scratch = [
        pltpu.VMEM(query_grad.shape, BF),
        pltpu.VMEM((heads, batch), BF),
        pltpu.VMEM(attn_input.shape, BF),
        pltpu.VMEM(query_weight.shape, F32),
        pltpu.VMEM((2, slots, local, units), BF),
        pltpu.VMEM((2, slots, local, units), BF),
        pltpu.VMEM((2, local, width, units), BF),
        pltpu.VMEM((2, local, width, units), BF),
        pltpu.VMEM((2, local, units, width), BF),
        pltpu.VMEM((tokens, width), BF),
        pltpu.VMEM((local * NE, slots, tokens), BF),
        pltpu.VMEM((local * NE, slots, 1), F32),
        pltpu.VMEM((2, local * NE, slots, width), BF),
        pltpu.VMEM((2, local, NE, slots, width), BF),
        pltpu.VMEM((LANES, 2, NZ, rows, q_wide), BF),
        pltpu.VMEM((LANES, NZ - 1, 2, rows, q_wide), BF),
        pltpu.VMEM((LANES, rows, q_wide), BF),
        pltpu.VMEM((LANES, rows, q_wide), BF),
        pltpu.VMEM((LANES, 2, NZ, slots, h_wide), BF),
        pltpu.VMEM((LANES, NZ - 1, 2, slots, h_wide), BF),
        pltpu.VMEM((LANES, 2, NZ, slots, units), BF),
        pltpu.VMEM((local, 2, 2, NZ, slots, width), BF),
        pltpu.VMEM((2, NE, local, slots, width), BF),
        dma((8,)),
        dma((2, NE)),
        dma((2, NE)),
        dma((6,)),
        dma((6,)),
        dma((LANES, NZ - 1)),
        dma((LANES, NZ - 1)),
        dma((LANES,)),
        dma((LANES,)),
        dma((LANES, NZ - 1)),
        dma((LANES, NZ - 1)),
        dma((LANES, NZ - 1)),
        dma((LANES, NZ - 1)),
        dma((local, 2, 2, NZ)),
        dma((2, NE, local)),
    ]
    return pl.pallas_call(
        step_kernel,
        name="backward_step",
        out_shape=(
            jax.ShapeDtypeStruct((rows, model), F32),
            jax.ShapeDtypeStruct((tokens, width), F32),
        ),
        in_specs=[vmem, vmem, vmem] + [hbm] * 8,
        out_specs=(vmem, vmem),
        scratch_shapes=scratch,
        compiler_params=pltpu.CompilerParams(
            collective_id=0, has_side_effects=True, vmem_limit_bytes=58 << 20
        ),
    )(
        expert_ids.T,
        route_weights.T,
        moe_cotangent,
        query_grad,
        attn_input,
        query_weight,
        gate_saved,
        up_saved,
        gate_weight,
        up_weight,
        down_weight.reshape(local, 2, units, width),
    )


def solution(mesh):
    placed = (
        P("dp", None),
        P("dp", "expert"),
        P(("expert", "dp"), None),
        P("expert", "dp"),
        P("expert", None),
        P("expert", None),
        P("dp", "expert", None),
        P("dp", "expert", None),
        P("expert", "dp", None),
        P("expert", "dp", None),
        P("expert", None, "dp"),
    )
    return jax.shard_map(
        shards,
        mesh=mesh,
        in_specs=placed,
        out_specs=(P(("expert", "dp"), None), P("expert", "dp")),
        check_vma=False,
    )
```

```python
import functools

import jax
import jax.numpy as jnp
from jax import lax
from jax.experimental import pallas as pl
from jax.experimental.pallas import tpu as pltpu
from jax.sharding import PartitionSpec as P

STEP_RATE = 0.01
EPSILON = 1e-06
MESH = pl.DeviceIdType.MESH
NZ = 8
NE = 16
LANES = 4
RING_ORDER = (0, 2, 1, 3)
NT = (((1,), (1,)), ((), ()))
BF = jnp.bfloat16
F32 = jnp.float32


def remote(src, dst, send_sem, recv_sem, device):
    return pltpu.make_async_remote_copy(
        src_ref=src,
        dst_ref=dst,
        send_sem=send_sem,
        recv_sem=recv_sem,
        device_id=device,
        device_id_type=MESH,
    )


def sign(lane):
    return 1 if lane < 2 else -1


def step_kernel(
    ids_ref,
    route_ref,
    cot_ref,
    grad_hbm,
    input_hbm,
    weight_hbm,
    gate_hbm,
    up_hbm,
    gate_w_hbm,
    up_w_hbm,
    down_w_hbm,
    query_out,
    moe_out,
    grad_v,
    grad_t,
    input_v,
    weight_v,
    gate_v,
    up_v,
    gate_w,
    up_w,
    down_w,
    cot_in,
    onehot,
    picks_t,
    scale,
    outgoing,
    arrived,
    q_part,
    q_recv,
    q_give,
    q_take,
    h_part,
    h_recv,
    grads,
    result,
    returned,
    load_sem,
    disp_send,
    disp_recv,
    pair_send,
    pair_got,
    q_send,
    q_got,
    qx_send,
    qx_got,
    h_send,
    h_got,
    g_send,
    g_got,
    r_send,
    r_got,
):
    e = lax.axis_index("expert")
    d = lax.axis_index("dp")
    h = d // NZ
    z = lax.rem(d, NZ)
    twin_d = (1 - h) * NZ + z
    twin = (e, twin_d)
    ahead = (e, h * NZ + lax.rem(z + 1, NZ))
    behind = (e, h * NZ + lax.rem(z + NZ - 1, NZ))
    units = gate_w.shape[-1]
    slots = gate_v.shape[1]
    experts = 2 * NE
    tokens = ids_ref.shape[1]

    def toward(lane):
        return ahead if sign(lane) > 0 else behind

    def at_z(lane, hops):
        return lax.rem(z + 4 * NZ - sign(lane) * hops, NZ)

    own = pl.ds(pl.multiple_of(h * units, 128), units)
    other = pl.ds(pl.multiple_of((1 - h) * units, 128), units)
    q_wide = q_part.shape[-1]

    def strip(lane):
        at = pl.ds(lane * q_wide, q_wide)
        return (input_hbm.at[:, at], input_v.at[:, at])

    loads = [
        pltpu.make_async_copy(src, dst, load_sem.at[i])
        for i, (src, dst) in enumerate(
            (
                (grad_hbm, grad_v),
                strip(0),
                strip(2),
                strip(1),
                strip(3),
                (down_w_hbm.at[:, h], down_w.at[h]),
                (gate_hbm.at[:, :, own], gate_v.at[h]),
                (up_hbm.at[:, :, own], up_v.at[h]),
                (gate_w_hbm.at[:, :, own], gate_w.at[h]),
                (up_w_hbm.at[:, :, own], up_w.at[h]),
                (weight_hbm, weight_v),
            )
        )
    ]
    shares = [
        remote(src, dst, pair_send.at[i], pair_got.at[i], twin)
        for i, (src, dst) in enumerate(
            (
                (cot_ref, cot_in),
                (down_w_hbm.at[:, 1 - h], down_w.at[h]),
                (gate_hbm.at[:, :, other], gate_v.at[h]),
                (up_hbm.at[:, :, other], up_v.at[h]),
                (gate_w_hbm.at[:, :, other], gate_w.at[h]),
                (up_w_hbm.at[:, :, other], up_w.at[h]),
            )
        )
    ]
    for copy in loads:
        copy.start()

    barrier = pltpu.get_barrier_semaphore()

    for device in (twin, ahead, behind):
        pl.semaphore_signal(barrier, inc=1, device_id=device, device_id_type=MESH)

    @pl.loop(1, NE)
    def _(k):
        for column in (d, twin_d):
            pl.semaphore_signal(
                barrier, inc=1, device_id=(lax.rem(e + k, NE), column), device_id_type=MESH
            )

    which = lax.broadcasted_iota(jnp.int32, (experts, tokens), 0)
    chosen = jnp.zeros((experts, tokens), F32)
    share = jnp.zeros((experts, tokens), F32)
    for k in range(ids_ref.shape[0]):
        hit = ids_ref[k : k + 1, :] == which
        chosen = chosen + jnp.where(hit, 1.0, 0.0)
        share = share + jnp.where(hit, route_ref[k : k + 1, :], 0.0)
    earlier = lax.broadcasted_iota(jnp.int32, (tokens, tokens), 0) < lax.broadcasted_iota(
        jnp.int32, (tokens, tokens), 1
    )
    before = jnp.dot(
        chosen.astype(BF), jnp.where(earlier, 1.0, 0.0).astype(BF), preferred_element_type=F32
    )
    position = jnp.where(chosen > 0.5, before, -1.0).astype(jnp.int32)
    slot_iota = lax.broadcasted_iota(jnp.int32, (slots, tokens), 0)
    for block in range(experts):
        mine = position[block : block + 1, :] == slot_iota
        scale[block] = jnp.sum(
            jnp.where(mine, share[block : block + 1, :], 0.0), axis=1, keepdims=True
        )
        onehot[block] = jnp.where(mine, 1.0, 0.0).astype(BF)

    def fill(side, cot):
        group = 8
        for first in range(0, experts, group):
            picks = onehot[first : first + group].reshape(group * slots, tokens)
            rows = jnp.dot(picks, cot, preferred_element_type=F32)
            rows = rows * scale[first : first + group].reshape(group * slots, 1)
            outgoing[side, first : first + group] = rows.astype(BF).reshape(group, slots, -1)

    def dispatch(side, k):
        to = lax.rem(e + k, NE)
        return remote(
            outgoing.at[side, pl.ds(2 * to, 2)],
            arrived.at[side, :, e],
            disp_send.at[side],
            disp_recv.at[side],
            (to, d),
        )

    def dispatch_all(side):
        @pl.loop(1, NE)
        def _(k):
            dispatch(side, k).start()

        arrived[side, :, e] = outgoing[side, pl.ds(2 * e, 2)]

    def ring(part, recv, send, got, lane, t):
        src = part.at[lane, :, at_z(lane, 1)] if isinstance(t, int) else recv.at[lane, t - 1]
        return remote(src, recv.at[lane, t], send, got.at[lane, t], toward(lane))

    def await_step(recv, send, got, lane, t):
        at = recv.at[lane, t]
        remote(at, at, send, got.at[lane, t], toward(lane)).wait_recv()

    def forward(part, recv, send, got, t):
        for lane in RING_ORDER:
            await_step(recv, send, got, lane, t - 1)
            total = recv[lane, t - 1].astype(F32) + part[lane, :, at_z(lane, 1 + t)].astype(F32)
            recv[lane, t - 1] = total.astype(BF)
            ring(part, recv, send, got, lane, t).start()

    def q_forward(t):
        forward(q_part, q_recv, q_send, q_got, t)

    def h_forward(t):
        forward(h_part, h_recv, h_send, h_got, t)

    def q_product(lane):
        @pl.loop(0, q_wide // 256)
        def _(j):
            columns = pl.ds(pl.multiple_of(lane * q_wide + j * 256, 256), 256)
            part = jnp.dot(grad_t[...], input_v[:, columns], preferred_element_type=F32)
            q_part[lane, :, :, :, pl.ds(pl.multiple_of(j * 256, 256), 256)] = part.astype(
                BF
            ).reshape(2, NZ, 32, 256)

    loads[0].wait()
    grad_t[...] = grad_v[...].T
    for i in (1, 2):
        loads[i].wait()
    for lane in (0, 2):
        q_product(lane)

    pl.semaphore_wait(barrier, 2 * NE + 1)
    shares[0].start()
    for lane in (0, 2):
        ring(q_part, q_recv, q_send, q_got, lane, 0).start()
    fill(h, cot_ref[...])
    dispatch_all(h)
    shares[1].start()
    shares[0].wait_recv()
    fill(1 - h, cot_in[...])
    dispatch_all(1 - h)
    for i in (3, 4):
        loads[i].wait()
    for lane in (1, 3):
        q_product(lane)
        ring(q_part, q_recv, q_send, q_got, lane, 0).start()

    @pl.loop(1, 5)
    def _(t):
        q_forward(t)

    shares[1].wait_recv()
    for copy in shares[2:]:
        copy.start()

    others = pl.ds(0, NE - 1)
    for side in range(2):
        at = arrived.at[side, :, others]
        remote(at, at, disp_send.at[side], disp_recv.at[side], twin).wait_recv()

    loads[5].wait()
    h_wide = h_part.shape[-1]
    for lane in RING_ORDER:
        expert, half = lane // 2, lane % 2
        rows = slice(half * h_wide, (half + 1) * h_wide)

        @pl.loop(0, 2)
        def _(block_side):
            part = 0.0
            for side in range(2):
                part = part + lax.dot_general(
                    arrived[side, expert, pl.ds(block_side * NZ, NZ)].reshape(NZ * slots, -1),
                    down_w[side, expert, rows, :],
                    NT,
                    preferred_element_type=F32,
                )
            h_part[lane, block_side] = part.astype(BF).reshape(NZ, slots, h_wide)

        ring(h_part, h_recv, h_send, h_got, lane, 0).start()

    @pl.loop(0, 2)
    def _(p):
        h_forward(2 * p + 1)
        h_forward(2 * p + 2)
        q_forward(p + 5)

    @pl.loop(5, NZ - 1)
    def _(t):
        h_forward(t)

    last = NZ - 2

    def gather(lane, t):
        at = grads.at[lane, :, at_z(lane, t)]
        return remote(at, at, g_send, g_got.at[lane, t], toward(lane))

    for i in (6, 7, 8, 9, 10):
        loads[i].wait()
    for i in (2, 3):
        shares[i].wait_recv()
    for expert in range(2):
        for half in range(2):
            lane = 2 * expert + half
            await_step(h_recv, h_send, h_got, lane, last)
            columns = slice(half * h_wide, (half + 1) * h_wide)
            for side in range(2):
                hidden = h_recv[lane, last, side].astype(F32) + h_part[lane, side, z].astype(F32)
                g = gate_v[side, :, expert, columns].astype(F32)
                u = up_v[side, :, expert, columns].astype(F32)
                sigma = 1.0 / (1.0 + jnp.exp(-g))
                grads[2 * expert, side, z, :, columns] = (
                    hidden * u * sigma * (1.0 + g * (1.0 - sigma))
                ).astype(BF)
                grads[2 * expert + 1, side, z, :, columns] = (hidden * g * sigma).astype(BF)
        for lane in (2 * expert, 2 * expert + 1):
            gather(lane, 0).start()

    def exchange(lane):
        return remote(q_give.at[lane], q_take.at[lane], qx_send.at[lane], qx_got.at[lane], twin)

    for lane in range(LANES):
        await_step(q_recv, q_send, q_got, lane, last)
        theirs = q_recv[lane, last, 1 - h].astype(F32) + q_part[lane, 1 - h, z].astype(F32)
        q_give[lane] = theirs.astype(BF)
        exchange(lane).start()

    def place(expert, width, side, block):
        return ((expert * 2 + width) * 2 + side) * NZ + block

    def reply(expert, width, side, block):
        return remote(
            result.at[place(expert, width, side, block)],
            returned.at[h, e, expert],
            r_send,
            r_got,
            (side * NZ + block, width * NZ + z),
        )

    def relay(t, lanes=RING_ORDER):
        for lane in lanes:
            gather(lane, t).wait_recv()
            gather(lane, t + 1).start()

    def produce(expert, *hops):
        blocks = [at_z(2 * expert, hop) for hop in hops]

        def rows_of(lane):
            parts = [grads[lane, :, block].reshape(2 * slots, units) for block in blocks]
            return jnp.concatenate(parts, axis=0)

        gate, up = rows_of(2 * expert), rows_of(2 * expert + 1)
        for width in range(2):
            rows = lax.dot_general(gate, gate_w[width, expert], NT, preferred_element_type=F32)
            rows = rows + lax.dot_general(
                up, up_w[width, expert], NT, preferred_element_type=F32
            )
            rows = rows.astype(BF).reshape(len(blocks), 2, slots, -1)
            for i, block in enumerate(blocks):
                for side in range(2):
                    at = place(expert, width, side, block)
                    result[at] = rows[i, side]
                    here = (side * NZ + block == e) & (width == h)

                    @pl.when(here)
                    def _():
                        pltpu.make_async_copy(
                            result.at[at], returned.at[h, e, expert], r_got
                        ).start()

                    @pl.when(jnp.logical_not(here))
                    def _():
                        reply(expert, width, side, block).start()

    @pl.loop(0, 4)
    def _(t):
        relay(t)

    picks_t[...] = onehot[...].reshape(experts * slots, tokens).T
    for i in (4, 5):
        shares[i].wait_recv()
    produce(0, 0, 1)
    relay(jnp.int32(4), (0, 2))
    produce(1, 0, 1)
    relay(jnp.int32(4), (1, 3))
    produce(0, 2, 3)
    relay(jnp.int32(5), (0, 2))
    produce(1, 2, 3)
    relay(jnp.int32(5), (1, 3))
    for expert in range(2):
        produce(expert, 4, 5)
    for expert in range(2):
        produce(expert, 6)

    for lane in range(LANES):
        exchange(lane).wait_recv()
        mine = q_recv[lane, last, h].astype(F32) + q_part[lane, h, z].astype(F32)
        query_out[:, lane * q_wide : (lane + 1) * q_wide] = mine + q_take[lane].astype(F32)
    gradient = query_out[...]
    weight = weight_v[...]
    count = 1.0 / weight.shape[1]
    radial = (jnp.sum(weight * gradient, axis=1, keepdims=True) * count) / (
        jnp.sum(weight * weight, axis=1, keepdims=True) * count + EPSILON
    )
    stepped = weight - STEP_RATE * (gradient - radial * weight)
    norm = jnp.sum(stepped * stepped, axis=1, keepdims=True) * count + EPSILON
    query_out[...] = stepped * lax.rsqrt(norm)
    for copy in shares:
        copy.wait_send()
    for side in range(2):
        at = outgoing.at[side, pl.ds(0, 2 * NE - 2)]
        remote(at, at, disp_send.at[side], disp_recv.at[side], twin).wait_send()
    for recv, send, got in ((q_recv, q_send, q_got), (h_recv, h_send, h_got)):
        remote(recv, recv, send, got.at[0, 0], twin).wait_send()
    for lane in range(LANES):
        exchange(lane).wait_send()

    for expert in range(2):
        for lane in (2 * expert, 2 * expert + 1):
            gather(lane, NZ - 2).wait_recv()
        produce(expert, NZ - 1)

    remote(returned, returned, r_send, r_got, twin).wait_recv()
    moe_out[...] = sum(
        jnp.dot(
            picks_t[...],
            returned[half].reshape(experts * slots, -1),
            preferred_element_type=F32,
        )
        for half in range(2)
    )

    at = grads.at[:, :, pl.ds(0, NZ - 1)]
    remote(at, at, g_send, g_got.at[0, 0], twin).wait_send()
    at = result.at[pl.ds(0, result.shape[0] - 2)]
    remote(at, at, r_send, r_got, twin).wait_send()


def shards(
    attn_input,
    query_grad,
    query_weight,
    moe_cotangent,
    expert_ids,
    route_weights,
    gate_saved,
    up_saved,
    gate_weight,
    up_weight,
    down_weight,
):
    vmem = pl.BlockSpec(memory_space=pltpu.VMEM)
    hbm = pl.BlockSpec(memory_space=pl.ANY)
    dma = pltpu.SemaphoreType.DMA
    tokens, width = moe_cotangent.shape
    slots, local, hidden = gate_saved.shape
    rows, model = query_weight.shape
    batch, heads = query_grad.shape
    units = hidden // 2
    q_wide, h_wide = model // LANES, local * units // LANES
    scratch = [
        pltpu.VMEM(query_grad.shape, BF),
        pltpu.VMEM((heads, batch), BF),
        pltpu.VMEM(attn_input.shape, BF),
        pltpu.VMEM(query_weight.shape, F32),
        pltpu.VMEM((2, slots, local, units), BF),
        pltpu.VMEM((2, slots, local, units), BF),
        pltpu.VMEM((2, local, width, units), BF),
        pltpu.VMEM((2, local, width, units), BF),
        pltpu.VMEM((2, local, units, width), BF),
        pltpu.VMEM((tokens, width), BF),
        pltpu.VMEM((local * NE, slots, tokens), BF),
        pltpu.VMEM((tokens, local * NE * slots), BF),
        pltpu.VMEM((local * NE, slots, 1), F32),
        pltpu.VMEM((2, local * NE, slots, width), BF),
        pltpu.VMEM((2, local, NE, slots, width), BF),
        pltpu.VMEM((LANES, 2, NZ, rows, q_wide), BF),
        pltpu.VMEM((LANES, NZ - 1, 2, rows, q_wide), BF),
        pltpu.VMEM((LANES, rows, q_wide), BF),
        pltpu.VMEM((LANES, rows, q_wide), BF),
        pltpu.VMEM((LANES, 2, NZ, slots, h_wide), BF),
        pltpu.VMEM((LANES, NZ - 1, 2, slots, h_wide), BF),
        pltpu.VMEM((LANES, 2, NZ, slots, units), BF),
        pltpu.VMEM((local * 4 * NZ, slots, width), BF),
        pltpu.VMEM((2, NE, local, slots, width), BF),
        dma((11,)),
        dma((2,)),
        dma((2,)),
        dma((6,)),
        dma((6,)),
        dma,
        dma((LANES, NZ - 1)),
        dma((LANES,)),
        dma((LANES,)),
        dma,
        dma((LANES, NZ - 1)),
        dma,
        dma((LANES, NZ - 1)),
        dma,
        dma,
    ]
    return pl.pallas_call(
        step_kernel,
        name="backward_step",
        out_shape=(
            jax.ShapeDtypeStruct((rows, model), F32),
            jax.ShapeDtypeStruct((tokens, width), F32),
        ),
        in_specs=[vmem, vmem, vmem] + [hbm] * 8,
        out_specs=(vmem, vmem),
        scratch_shapes=scratch,
        compiler_params=pltpu.CompilerParams(
            collective_id=0, has_side_effects=True, vmem_limit_bytes=58 << 20
        ),
    )(
        expert_ids.T,
        route_weights.T,
        moe_cotangent,
        query_grad,
        attn_input,
        query_weight,
        gate_saved,
        up_saved,
        gate_weight,
        up_weight,
        down_weight.reshape(local, 2, units, width),
    )


def solution(mesh):
    placed = (
        P("dp", None),
        P("dp", "expert"),
        P(("expert", "dp"), None),
        P("expert", "dp"),
        P("expert", None),
        P("expert", None),
        P("dp", "expert", None),
        P("dp", "expert", None),
        P("expert", "dp", None),
        P("expert", "dp", None),
        P("expert", None, "dp"),
    )
    return jax.shard_map(
        shards,
        mesh=mesh,
        in_specs=placed,
        out_specs=(P(("expert", "dp"), None), P("expert", "dp")),
        check_vma=False,
    )
```

```python
import functools

import jax
import jax.numpy as jnp
from jax import lax
from jax.experimental import pallas as pl
from jax.experimental.pallas import tpu as pltpu
from jax.sharding import PartitionSpec as P

STEP_RATE = 0.01
EPSILON = 1e-06
MESH = pl.DeviceIdType.MESH
NZ = 8
NE = 16
LANES = 4
LONG = ((0, 1, 4), (2, -1, 4), (1, 1, 4), (3, -1, 4))
SHORT = ((0, -1, 3), (2, 1, 3), (1, -1, 3), (3, 1, 3))
CHAINS = LONG + SHORT
NT = (((1,), (1,)), ((), ()))
BF = jnp.bfloat16
F32 = jnp.float32


def remote(src, dst, send_sem, recv_sem, device):
    return pltpu.make_async_remote_copy(
        src_ref=src,
        dst_ref=dst,
        send_sem=send_sem,
        recv_sem=recv_sem,
        device_id=device,
        device_id_type=MESH,
    )


def slot(way, t):
    return t if way > 0 else NZ // 2 + t


def step_kernel(
    ids_ref,
    route_ref,
    cot_ref,
    grad_hbm,
    input_hbm,
    weight_hbm,
    gate_hbm,
    up_hbm,
    gate_w_hbm,
    up_w_hbm,
    down_w_hbm,
    query_out,
    moe_out,
    grad_v,
    grad_t,
    input_v,
    weight_v,
    gate_v,
    up_v,
    gate_w,
    up_w,
    down_w,
    cot_in,
    onehot,
    picks_t,
    scale,
    outgoing,
    arrived,
    q_part,
    q_recv,
    q_give,
    q_take,
    h_part,
    h_recv,
    grads,
    result,
    returned,
    load_sem,
    disp_send,
    disp_recv,
    pair_send,
    pair_got,
    q_send,
    q_got,
    qx_send,
    qx_got,
    h_send,
    h_got,
    g_send,
    g_got,
    r_send,
    r_got,
):
    e = lax.axis_index("expert")
    d = lax.axis_index("dp")
    h = d // NZ
    z = lax.rem(d, NZ)
    twin_d = (1 - h) * NZ + z
    twin = (e, twin_d)
    ahead = (e, h * NZ + lax.rem(z + 1, NZ))
    behind = (e, h * NZ + lax.rem(z + NZ - 1, NZ))
    units = gate_w.shape[-1]
    slots = gate_v.shape[1]
    experts = 2 * NE
    tokens = ids_ref.shape[1]

    def toward(way):
        return ahead if way > 0 else behind

    def at_z(offset):
        return lax.rem(z + 2 * NZ + offset, NZ)

    own = pl.ds(pl.multiple_of(h * units, 128), units)
    other = pl.ds(pl.multiple_of((1 - h) * units, 128), units)
    q_wide = q_part.shape[-1]

    def strip(lane):
        at = pl.ds(lane * q_wide, q_wide)
        return (input_hbm.at[:, at], input_v.at[:, at])

    loads = [
        pltpu.make_async_copy(src, dst, load_sem.at[i])
        for i, (src, dst) in enumerate(
            (
                (grad_hbm, grad_v),
                strip(0),
                strip(2),
                strip(1),
                strip(3),
                (down_w_hbm.at[:, h], down_w.at[h]),
                (gate_hbm.at[:, :, own], gate_v.at[h]),
                (up_hbm.at[:, :, own], up_v.at[h]),
                (gate_w_hbm.at[:, :, own], gate_w.at[h]),
                (up_w_hbm.at[:, :, own], up_w.at[h]),
                (weight_hbm, weight_v),
            )
        )
    ]
    shares = [
        remote(src, dst, pair_send.at[i], pair_got.at[i], twin)
        for i, (src, dst) in enumerate(
            (
                (cot_ref, cot_in),
                (down_w_hbm.at[:, 1 - h], down_w.at[h]),
                (gate_hbm.at[:, :, other], gate_v.at[h]),
                (up_hbm.at[:, :, other], up_v.at[h]),
                (gate_w_hbm.at[:, :, other], gate_w.at[h]),
                (up_w_hbm.at[:, :, other], up_w.at[h]),
            )
        )
    ]
    for copy in loads:
        copy.start()

    barrier = pltpu.get_barrier_semaphore()

    for device in (twin, ahead, behind):
        pl.semaphore_signal(barrier, inc=1, device_id=device, device_id_type=MESH)

    @pl.loop(1, NE)
    def _(k):
        for column in (d, twin_d):
            pl.semaphore_signal(
                barrier, inc=1, device_id=(lax.rem(e + k, NE), column), device_id_type=MESH
            )

    which = lax.broadcasted_iota(jnp.int32, (experts, tokens), 0)
    chosen = jnp.zeros((experts, tokens), F32)
    share = jnp.zeros((experts, tokens), F32)
    for k in range(ids_ref.shape[0]):
        hit = ids_ref[k : k + 1, :] == which
        chosen = chosen + jnp.where(hit, 1.0, 0.0)
        share = share + jnp.where(hit, route_ref[k : k + 1, :], 0.0)
    earlier = lax.broadcasted_iota(jnp.int32, (tokens, tokens), 0) < lax.broadcasted_iota(
        jnp.int32, (tokens, tokens), 1
    )
    before = jnp.dot(
        chosen.astype(BF), jnp.where(earlier, 1.0, 0.0).astype(BF), preferred_element_type=F32
    )
    position = jnp.where(chosen > 0.5, before, -1.0).astype(jnp.int32)
    slot_iota = lax.broadcasted_iota(jnp.int32, (slots, tokens), 0)
    for block in range(experts):
        mine = position[block : block + 1, :] == slot_iota
        scale[block] = jnp.sum(
            jnp.where(mine, share[block : block + 1, :], 0.0), axis=1, keepdims=True
        )
        onehot[block] = jnp.where(mine, 1.0, 0.0).astype(BF)

    def fill(side, cot):
        group = 8
        for first in range(0, experts, group):
            picks = onehot[first : first + group].reshape(group * slots, tokens)
            rows = jnp.dot(picks, cot, preferred_element_type=F32)
            rows = rows * scale[first : first + group].reshape(group * slots, 1)
            outgoing[side, first : first + group] = rows.astype(BF).reshape(group, slots, -1)

    def dispatch(side, k):
        to = lax.rem(e + k, NE)
        return remote(
            outgoing.at[side, pl.ds(2 * to, 2)],
            arrived.at[side, :, e],
            disp_send.at[side],
            disp_recv.at[side],
            (to, d),
        )

    def dispatch_all(side):
        @pl.loop(1, NE)
        def _(k):
            dispatch(side, k).start()

        arrived[side, :, e] = outgoing[side, pl.ds(2 * e, 2)]

    def ring(part, recv, send, got, chain, t):
        lane, way, hops = chain
        src = part.at[lane, :, at_z(way * hops)] if t == 0 else recv.at[lane, slot(way, t - 1)]
        at = slot(way, t)
        return remote(src, recv.at[lane, at], send, got.at[lane, at], toward(way))

    def await_step(recv, send, got, chain, t):
        lane, way, _ = chain
        at = recv.at[lane, slot(way, t)]
        remote(at, at, send, got.at[lane, slot(way, t)], toward(way)).wait_recv()

    def begin(part, recv, send, got, lane):
        for chain in CHAINS:
            if chain[0] == lane:
                ring(part, recv, send, got, chain, 0).start()

    def forward(part, recv, send, got, t):
        for chain in CHAINS if t < 3 else LONG:
            lane, way, hops = chain
            await_step(recv, send, got, chain, t - 1)
            at = slot(way, t - 1)
            own_part = part[lane, :, at_z(way * (hops - t))]
            recv[lane, at] = (recv[lane, at].astype(F32) + own_part.astype(F32)).astype(BF)
            ring(part, recv, send, got, chain, t).start()

    def finish(recv, send, got, lane):
        for chain in CHAINS:
            if chain[0] == lane:
                await_step(recv, send, got, chain, chain[2] - 1)

    def summed(part, recv, lane, side):
        long = 1 if lane < 2 else -1
        both = recv[lane, slot(long, 3), side].astype(F32)
        both = both + recv[lane, slot(-long, 2), side].astype(F32)
        return both + part[lane, side, z].astype(F32)

    def q_forward(t):
        forward(q_part, q_recv, q_send, q_got, t)

    def h_forward(t):
        forward(h_part, h_recv, h_send, h_got, t)

    def q_product(lane):
        @pl.loop(0, q_wide // 256)
        def _(j):
            columns = pl.ds(pl.multiple_of(lane * q_wide + j * 256, 256), 256)
            part = jnp.dot(grad_t[...], input_v[:, columns], preferred_element_type=F32)
            q_part[lane, :, :, :, pl.ds(pl.multiple_of(j * 256, 256), 256)] = part.astype(
                BF
            ).reshape(2, NZ, 32, 256)

    loads[0].wait()
    grad_t[...] = grad_v[...].T
    for i in (1, 2):
        loads[i].wait()
    for lane in (0, 2):
        q_product(lane)

    pl.semaphore_wait(barrier, 2 * NE + 1)
    shares[0].start()
    for lane in (0, 2):
        begin(q_part, q_recv, q_send, q_got, lane)
    fill(h, cot_ref[...])
    dispatch_all(h)
    shares[1].start()
    shares[0].wait_recv()
    fill(1 - h, cot_in[...])
    dispatch_all(1 - h)
    for i in (3, 4):
        loads[i].wait()
    for lane in (1, 3):
        q_product(lane)
        begin(q_part, q_recv, q_send, q_got, lane)

    q_forward(1)
    q_forward(2)
    shares[1].wait_recv()
    for copy in shares[2:]:
        copy.start()

    others = pl.ds(0, NE - 1)
    for side in range(2):
        at = arrived.at[side, :, others]
        remote(at, at, disp_send.at[side], disp_recv.at[side], twin).wait_recv()

    loads[5].wait()
    h_wide = h_part.shape[-1]
    for lane in range(LANES):
        expert, half = lane // 2, lane % 2
        rows = slice(half * h_wide, (half + 1) * h_wide)

        @pl.loop(0, 2)
        def _(block_side):
            part = 0.0
            for side in range(2):
                part = part + lax.dot_general(
                    arrived[side, expert, pl.ds(block_side * NZ, NZ)].reshape(NZ * slots, -1),
                    down_w[side, expert, rows, :],
                    NT,
                    preferred_element_type=F32,
                )
            h_part[lane, block_side] = part.astype(BF).reshape(NZ, slots, h_wide)

        begin(h_part, h_recv, h_send, h_got, lane)

    h_forward(1)
    q_forward(3)
    h_forward(2)
    h_forward(3)

    def gather(chain, t):
        lane, way, _ = chain
        at = grads.at[lane, :, at_z(-way * t)]
        return remote(at, at, g_send, g_got.at[lane, slot(way, t)], toward(way))

    for i in (6, 7, 8, 9, 10):
        loads[i].wait()
    for i in (2, 3):
        shares[i].wait_recv()
    for expert in range(2):
        for half in range(2):
            lane = 2 * expert + half
            finish(h_recv, h_send, h_got, lane)
            columns = slice(half * h_wide, (half + 1) * h_wide)
            for side in range(2):
                hidden = summed(h_part, h_recv, lane, side)
                g = gate_v[side, :, expert, columns].astype(F32)
                u = up_v[side, :, expert, columns].astype(F32)
                sigma = 1.0 / (1.0 + jnp.exp(-g))
                grads[2 * expert, side, z, :, columns] = (
                    hidden * u * sigma * (1.0 + g * (1.0 - sigma))
                ).astype(BF)
                grads[2 * expert + 1, side, z, :, columns] = (hidden * g * sigma).astype(BF)
        for chain in CHAINS:
            if chain[0] // 2 == expert:
                gather(chain, 0).start()

    def exchange(lane):
        return remote(q_give.at[lane], q_take.at[lane], qx_send.at[lane], qx_got.at[lane], twin)

    for lane in range(LANES):
        finish(q_recv, q_send, q_got, lane)
        q_give[lane] = summed(q_part, q_recv, lane, 1 - h).astype(BF)
        exchange(lane).start()

    def place(expert, width, side, block):
        return ((expert * 2 + width) * 2 + side) * NZ + block

    def reply(expert, width, side, block):
        return remote(
            result.at[place(expert, width, side, block)],
            returned.at[h, e, expert],
            r_send,
            r_got,
            (side * NZ + block, width * NZ + z),
        )

    def relay(t, chains=CHAINS):
        for chain in chains:
            gather(chain, t).wait_recv()
            if t + 1 < chain[2]:
                gather(chain, t + 1).start()

    def produce(expert, *offsets):
        blocks = [at_z(offset) for offset in offsets]

        def rows_of(lane):
            parts = [grads[lane, :, block].reshape(2 * slots, units) for block in blocks]
            return jnp.concatenate(parts, axis=0)

        gate, up = rows_of(2 * expert), rows_of(2 * expert + 1)
        for width in range(2):
            rows = lax.dot_general(gate, gate_w[width, expert], NT, preferred_element_type=F32)
            rows = rows + lax.dot_general(
                up, up_w[width, expert], NT, preferred_element_type=F32
            )
            rows = rows.astype(BF).reshape(len(blocks), 2, slots, -1)
            for i, block in enumerate(blocks):
                for side in range(2):
                    at = place(expert, width, side, block)
                    result[at] = rows[i, side]
                    here = (side * NZ + block == e) & (width == h)

                    @pl.when(here)
                    def _():
                        pltpu.make_async_copy(
                            result.at[at], returned.at[h, e, expert], r_got
                        ).start()

                    @pl.when(jnp.logical_not(here))
                    def _():
                        reply(expert, width, side, block).start()

    relay(0)
    picks_t[...] = onehot[...].reshape(experts * slots, tokens).T
    relay(1)

    for lane in range(LANES):
        exchange(lane).wait_recv()
        mine = summed(q_part, q_recv, lane, h)
        query_out[:, lane * q_wide : (lane + 1) * q_wide] = mine + q_take[lane].astype(F32)
    gradient = query_out[...]
    weight = weight_v[...]
    count = 1.0 / weight.shape[1]
    radial = (jnp.sum(weight * gradient, axis=1, keepdims=True) * count) / (
        jnp.sum(weight * weight, axis=1, keepdims=True) * count + EPSILON
    )
    stepped = weight - STEP_RATE * (gradient - radial * weight)
    norm = jnp.sum(stepped * stepped, axis=1, keepdims=True) * count + EPSILON
    query_out[...] = stepped * lax.rsqrt(norm)

    for i in (4, 5):
        shares[i].wait_recv()
    produce(0, 0, 1, -1)
    produce(1, 0, 1, -1)
    relay(2, LONG)
    produce(0, 2, -2)
    produce(1, 2, -2)
    relay(2, SHORT)
    produce(0, 3, -3)
    produce(1, 3, -3)
    for copy in shares:
        copy.wait_send()
    for side in range(2):
        at = outgoing.at[side, pl.ds(0, 2 * NE - 2)]
        remote(at, at, disp_send.at[side], disp_recv.at[side], twin).wait_send()
    for recv, send, got in ((q_recv, q_send, q_got), (h_recv, h_send, h_got)):
        at = recv.at[:, pl.ds(0, NZ - 1)]
        remote(at, at, send, got.at[0, 0], twin).wait_send()
    for lane in range(LANES):
        exchange(lane).wait_send()

    for expert in range(2):
        relay(3, [chain for chain in LONG if chain[0] // 2 == expert])
        produce(expert, 4)

    remote(returned, returned, r_send, r_got, twin).wait_recv()
    moe_out[...] = sum(
        jnp.dot(
            picks_t[...],
            returned[half].reshape(experts * slots, -1),
            preferred_element_type=F32,
        )
        for half in range(2)
    )

    at = grads.at[:, :, pl.ds(0, NZ - 1)]
    remote(at, at, g_send, g_got.at[0, 0], twin).wait_send()
    at = result.at[pl.ds(0, result.shape[0] - 2)]
    remote(at, at, r_send, r_got, twin).wait_send()


def shards(
    attn_input,
    query_grad,
    query_weight,
    moe_cotangent,
    expert_ids,
    route_weights,
    gate_saved,
    up_saved,
    gate_weight,
    up_weight,
    down_weight,
):
    vmem = pl.BlockSpec(memory_space=pltpu.VMEM)
    hbm = pl.BlockSpec(memory_space=pl.ANY)
    dma = pltpu.SemaphoreType.DMA
    tokens, width = moe_cotangent.shape
    slots, local, hidden = gate_saved.shape
    rows, model = query_weight.shape
    batch, heads = query_grad.shape
    units = hidden // 2
    q_wide, h_wide = model // LANES, local * units // LANES
    scratch = [
        pltpu.VMEM(query_grad.shape, BF),
        pltpu.VMEM((heads, batch), BF),
        pltpu.VMEM(attn_input.shape, BF),
        pltpu.VMEM(query_weight.shape, F32),
        pltpu.VMEM((2, slots, local, units), BF),
        pltpu.VMEM((2, slots, local, units), BF),
        pltpu.VMEM((2, local, width, units), BF),
        pltpu.VMEM((2, local, width, units), BF),
        pltpu.VMEM((2, local, units, width), BF),
        pltpu.VMEM((tokens, width), BF),
        pltpu.VMEM((local * NE, slots, tokens), BF),
        pltpu.VMEM((tokens, local * NE * slots), BF),
        pltpu.VMEM((local * NE, slots, 1), F32),
        pltpu.VMEM((2, local * NE, slots, width), BF),
        pltpu.VMEM((2, local, NE, slots, width), BF),
        pltpu.VMEM((LANES, 2, NZ, rows, q_wide), BF),
        pltpu.VMEM((LANES, NZ, 2, rows, q_wide), BF),
        pltpu.VMEM((LANES, rows, q_wide), BF),
        pltpu.VMEM((LANES, rows, q_wide), BF),
        pltpu.VMEM((LANES, 2, NZ, slots, h_wide), BF),
        pltpu.VMEM((LANES, NZ, 2, slots, h_wide), BF),
        pltpu.VMEM((LANES, 2, NZ, slots, units), BF),
        pltpu.VMEM((local * 4 * NZ, slots, width), BF),
        pltpu.VMEM((2, NE, local, slots, width), BF),
        dma((11,)),
        dma((2,)),
        dma((2,)),
        dma((6,)),
        dma((6,)),
        dma,
        dma((LANES, NZ)),
        dma((LANES,)),
        dma((LANES,)),
        dma,
        dma((LANES, NZ)),
        dma,
        dma((LANES, NZ)),
        dma,
        dma,
    ]
    return pl.pallas_call(
        step_kernel,
        name="backward_step",
        out_shape=(
            jax.ShapeDtypeStruct((rows, model), F32),
            jax.ShapeDtypeStruct((tokens, width), F32),
        ),
        in_specs=[vmem, vmem, vmem] + [hbm] * 8,
        out_specs=(vmem, vmem),
        scratch_shapes=scratch,
        compiler_params=pltpu.CompilerParams(
            collective_id=0, has_side_effects=True, vmem_limit_bytes=58 << 20
        ),
    )(
        expert_ids.T,
        route_weights.T,
        moe_cotangent,
        query_grad,
        attn_input,
        query_weight,
        gate_saved,
        up_saved,
        gate_weight,
        up_weight,
        down_weight.reshape(local, 2, units, width),
    )


def solution(mesh):
    placed = (
        P("dp", None),
        P("dp", "expert"),
        P(("expert", "dp"), None),
        P("expert", "dp"),
        P("expert", None),
        P("expert", None),
        P("dp", "expert", None),
        P("dp", "expert", None),
        P("expert", "dp", None),
        P("expert", "dp", None),
        P("expert", None, "dp"),
    )
    return jax.shard_map(
        shards,
        mesh=mesh,
        in_specs=placed,
        out_specs=(P(("expert", "dp"), None), P("expert", "dp")),
        check_vma=False,
    )
```

```python
import functools

import jax
import jax.numpy as jnp
from jax import lax
from jax.experimental import pallas as pl
from jax.experimental.pallas import tpu as pltpu
from jax.sharding import PartitionSpec as P

STEP_RATE = 0.01
EPSILON = 1e-06
MESH = pl.DeviceIdType.MESH
NZ = 8
NE = 16
LANES = 4
LONG = ((0, 1, 4), (2, -1, 4), (1, 1, 4), (3, -1, 4))
SHORT = ((0, -1, 3), (2, 1, 3), (1, -1, 3), (3, 1, 3))
CHAINS = LONG + SHORT
NT = (((1,), (1,)), ((), ()))
BF = jnp.bfloat16
F32 = jnp.float32


def remote(src, dst, send_sem, recv_sem, device):
    return pltpu.make_async_remote_copy(
        src_ref=src,
        dst_ref=dst,
        send_sem=send_sem,
        recv_sem=recv_sem,
        device_id=device,
        device_id_type=MESH,
    )


def slot(way, t):
    return t if way > 0 else NZ // 2 + t


def step_kernel(
    ids_ref,
    route_ref,
    cot_ref,
    grad_hbm,
    input_hbm,
    weight_hbm,
    gate_hbm,
    up_hbm,
    gate_w_hbm,
    up_w_hbm,
    down_w_hbm,
    query_out,
    moe_out,
    grad_v,
    grad_t,
    input_v,
    weight_v,
    gate_v,
    up_v,
    gate_w,
    up_w,
    down_w,
    cot_in,
    onehot,
    picks_t,
    scale,
    outgoing,
    arrived,
    q_part,
    q_recv,
    q_give,
    q_take,
    h_part,
    h_recv,
    grads,
    result,
    returned,
    load_sem,
    disp_send,
    disp_recv,
    pair_send,
    pair_got,
    q_send,
    q_got,
    qx_send,
    qx_got,
    h_send,
    h_got,
    g_send,
    g_got,
    r_send,
    r_got,
):
    e = lax.axis_index("expert")
    d = lax.axis_index("dp")
    h = d // NZ
    z = lax.rem(d, NZ)
    twin_d = (1 - h) * NZ + z
    twin = (e, twin_d)
    ahead = (e, h * NZ + lax.rem(z + 1, NZ))
    behind = (e, h * NZ + lax.rem(z + NZ - 1, NZ))
    units = gate_w.shape[-1]
    slots = gate_v.shape[1]
    experts = 2 * NE
    tokens = ids_ref.shape[1]

    def toward(way):
        return ahead if way > 0 else behind

    def at_z(offset):
        return lax.rem(z + 2 * NZ + offset, NZ)

    own = pl.ds(pl.multiple_of(h * units, 128), units)
    other = pl.ds(pl.multiple_of((1 - h) * units, 128), units)
    q_wide = q_part.shape[-1]

    def strip(lane):
        at = pl.ds(lane * q_wide, q_wide)
        return (input_hbm.at[:, at], input_v.at[:, at])

    loads = [
        pltpu.make_async_copy(src, dst, load_sem.at[i])
        for i, (src, dst) in enumerate(
            (
                (grad_hbm, grad_v),
                strip(0),
                strip(2),
                strip(1),
                strip(3),
                (down_w_hbm.at[:, h], down_w.at[h]),
                (gate_hbm.at[:, :, own], gate_v.at[h]),
                (up_hbm.at[:, :, own], up_v.at[h]),
                (gate_w_hbm.at[:, :, own], gate_w.at[h]),
                (up_w_hbm.at[:, :, own], up_w.at[h]),
                (weight_hbm, weight_v),
            )
        )
    ]
    shares = [
        remote(src, dst, pair_send.at[i], pair_got.at[i], twin)
        for i, (src, dst) in enumerate(
            (
                (cot_ref, cot_in),
                (down_w_hbm.at[:, 1 - h], down_w.at[h]),
                (gate_hbm.at[:, :, other], gate_v.at[h]),
                (up_hbm.at[:, :, other], up_v.at[h]),
                (gate_w_hbm.at[:, :, other], gate_w.at[h]),
                (up_w_hbm.at[:, :, other], up_w.at[h]),
            )
        )
    ]
    for copy in loads:
        copy.start()

    barrier = pltpu.get_barrier_semaphore()

    for device in (twin, ahead, behind):
        pl.semaphore_signal(barrier, inc=1, device_id=device, device_id_type=MESH)

    @pl.loop(1, NE)
    def _(k):
        for column in (d, twin_d):
            pl.semaphore_signal(
                barrier, inc=1, device_id=(lax.rem(e + k, NE), column), device_id_type=MESH
            )

    which = lax.broadcasted_iota(jnp.int32, (experts, tokens), 0)
    chosen = jnp.zeros((experts, tokens), F32)
    share = jnp.zeros((experts, tokens), F32)
    for k in range(ids_ref.shape[0]):
        hit = ids_ref[k : k + 1, :] == which
        chosen = chosen + jnp.where(hit, 1.0, 0.0)
        share = share + jnp.where(hit, route_ref[k : k + 1, :], 0.0)
    earlier = lax.broadcasted_iota(jnp.int32, (tokens, tokens), 0) < lax.broadcasted_iota(
        jnp.int32, (tokens, tokens), 1
    )
    before = jnp.dot(
        chosen.astype(BF), jnp.where(earlier, 1.0, 0.0).astype(BF), preferred_element_type=F32
    )
    position = jnp.where(chosen > 0.5, before, -1.0).astype(jnp.int32)
    slot_iota = lax.broadcasted_iota(jnp.int32, (slots, tokens), 0)
    for block in range(experts):
        mine = position[block : block + 1, :] == slot_iota
        scale[block] = jnp.sum(
            jnp.where(mine, share[block : block + 1, :], 0.0), axis=1, keepdims=True
        )
        onehot[block] = jnp.where(mine, 1.0, 0.0).astype(BF)

    def fill(side, cot):
        group = 8
        for first in range(0, experts, group):
            picks = onehot[first : first + group].reshape(group * slots, tokens)
            rows = jnp.dot(picks, cot, preferred_element_type=F32)
            rows = rows * scale[first : first + group].reshape(group * slots, 1)
            outgoing[side, first : first + group] = rows.astype(BF).reshape(group, slots, -1)

    def dispatch(side, k):
        to = lax.rem(e + k, NE)
        return remote(
            outgoing.at[side, pl.ds(2 * to, 2)],
            arrived.at[side, :, e],
            disp_send.at[side],
            disp_recv.at[side],
            (to, d),
        )

    def dispatch_all(side):
        @pl.loop(1, NE)
        def _(k):
            dispatch(side, k).start()

        arrived[side, :, e] = outgoing[side, pl.ds(2 * e, 2)]

    def ring(part, recv, send, got, chain, t):
        lane, way, hops = chain
        src = part.at[lane, :, at_z(way * hops)] if t == 0 else recv.at[lane, slot(way, t - 1)]
        at = slot(way, t)
        return remote(src, recv.at[lane, at], send, got.at[lane, at], toward(way))

    def await_step(recv, send, got, chain, t):
        lane, way, _ = chain
        at = recv.at[lane, slot(way, t)]
        remote(at, at, send, got.at[lane, slot(way, t)], toward(way)).wait_recv()

    def begin(part, recv, send, got, lane):
        for chain in CHAINS:
            if chain[0] == lane:
                ring(part, recv, send, got, chain, 0).start()

    def forward(part, recv, send, got, t):
        for chain in CHAINS if t < 3 else LONG:
            lane, way, hops = chain
            await_step(recv, send, got, chain, t - 1)
            at = slot(way, t - 1)
            own_part = part[lane, :, at_z(way * (hops - t))]
            recv[lane, at] = (recv[lane, at].astype(F32) + own_part.astype(F32)).astype(BF)
            ring(part, recv, send, got, chain, t).start()

    def finish(recv, send, got, lane):
        for chain in CHAINS:
            if chain[0] == lane:
                await_step(recv, send, got, chain, chain[2] - 1)

    def summed(part, recv, lane, side):
        long = 1 if lane < 2 else -1
        both = recv[lane, slot(long, 3), side].astype(F32)
        both = both + recv[lane, slot(-long, 2), side].astype(F32)
        return both + part[lane, side, z].astype(F32)

    def q_forward(t):
        forward(q_part, q_recv, q_send, q_got, t)

    def h_forward(t):
        forward(h_part, h_recv, h_send, h_got, t)

    def q_product(lane):
        @pl.loop(0, q_wide // 256)
        def _(j):
            columns = pl.ds(pl.multiple_of(lane * q_wide + j * 256, 256), 256)
            part = jnp.dot(grad_t[...], input_v[:, columns], preferred_element_type=F32)
            q_part[lane, :, :, :, pl.ds(pl.multiple_of(j * 256, 256), 256)] = part.astype(
                BF
            ).reshape(2, NZ, 32, 256)

    loads[0].wait()
    grad_t[...] = grad_v[...].T
    loads[1].wait()
    q_product(0)

    pl.semaphore_wait(barrier, 2 * NE + 1)
    shares[0].start()
    begin(q_part, q_recv, q_send, q_got, 0)
    fill(h, cot_ref[...])
    dispatch_all(h)
    shares[1].start()
    loads[2].wait()
    q_product(2)
    begin(q_part, q_recv, q_send, q_got, 2)
    shares[0].wait_recv()
    fill(1 - h, cot_in[...])
    dispatch_all(1 - h)
    for i in (3, 4):
        loads[i].wait()
    for lane in (1, 3):
        q_product(lane)
        begin(q_part, q_recv, q_send, q_got, lane)

    q_forward(1)
    q_forward(2)
    shares[1].wait_recv()
    for copy in shares[2:]:
        copy.start()

    others = pl.ds(0, NE - 1)
    for side in range(2):
        at = arrived.at[side, :, others]
        remote(at, at, disp_send.at[side], disp_recv.at[side], twin).wait_recv()

    loads[5].wait()
    h_wide = h_part.shape[-1]
    for lane in range(LANES):
        expert, half = lane // 2, lane % 2
        rows = slice(half * h_wide, (half + 1) * h_wide)

        @pl.loop(0, 2)
        def _(block_side):
            part = 0.0
            for side in range(2):
                part = part + lax.dot_general(
                    arrived[side, expert, pl.ds(block_side * NZ, NZ)].reshape(NZ * slots, -1),
                    down_w[side, expert, rows, :],
                    NT,
                    preferred_element_type=F32,
                )
            h_part[lane, block_side] = part.astype(BF).reshape(NZ, slots, h_wide)

        begin(h_part, h_recv, h_send, h_got, lane)

    h_forward(1)
    q_forward(3)
    h_forward(2)
    h_forward(3)

    def gather(chain, t):
        lane, way, _ = chain
        at = grads.at[lane, :, at_z(-way * t)]
        return remote(at, at, g_send, g_got.at[lane, slot(way, t)], toward(way))

    for i in (6, 7, 8, 9, 10):
        loads[i].wait()
    for i in (2, 3):
        shares[i].wait_recv()
    for expert in range(2):
        for half in range(2):
            lane = 2 * expert + half
            finish(h_recv, h_send, h_got, lane)
            columns = slice(half * h_wide, (half + 1) * h_wide)
            for side in range(2):
                hidden = summed(h_part, h_recv, lane, side)
                g = gate_v[side, :, expert, columns].astype(F32)
                u = up_v[side, :, expert, columns].astype(F32)
                sigma = 1.0 / (1.0 + jnp.exp(-g))
                grads[2 * expert, side, z, :, columns] = (
                    hidden * u * sigma * (1.0 + g * (1.0 - sigma))
                ).astype(BF)
                grads[2 * expert + 1, side, z, :, columns] = (hidden * g * sigma).astype(BF)
        for chain in CHAINS:
            if chain[0] // 2 == expert:
                gather(chain, 0).start()

    def exchange(lane):
        return remote(q_give.at[lane], q_take.at[lane], qx_send.at[lane], qx_got.at[lane], twin)

    for lane in range(LANES):
        finish(q_recv, q_send, q_got, lane)
        q_give[lane] = summed(q_part, q_recv, lane, 1 - h).astype(BF)
        exchange(lane).start()

    def place(expert, width, side, block):
        return ((expert * 2 + width) * 2 + side) * NZ + block

    def reply(expert, width, side, block):
        return remote(
            result.at[place(expert, width, side, block)],
            returned.at[h, e, expert],
            r_send,
            r_got,
            (side * NZ + block, width * NZ + z),
        )

    def relay(t, chains=CHAINS):
        for chain in chains:
            gather(chain, t).wait_recv()
            if t + 1 < chain[2]:
                gather(chain, t + 1).start()

    def produce(expert, *offsets):
        blocks = [at_z(offset) for offset in offsets]

        def rows_of(lane):
            parts = [grads[lane, :, block].reshape(2 * slots, units) for block in blocks]
            return jnp.concatenate(parts, axis=0)

        gate, up = rows_of(2 * expert), rows_of(2 * expert + 1)
        for width in range(2):
            rows = lax.dot_general(gate, gate_w[width, expert], NT, preferred_element_type=F32)
            rows = rows + lax.dot_general(
                up, up_w[width, expert], NT, preferred_element_type=F32
            )
            rows = rows.astype(BF).reshape(len(blocks), 2, slots, -1)
            for i, block in enumerate(blocks):
                for side in range(2):
                    at = place(expert, width, side, block)
                    result[at] = rows[i, side]
                    here = (side * NZ + block == e) & (width == h)

                    @pl.when(here)
                    def _():
                        pltpu.make_async_copy(
                            result.at[at], returned.at[h, e, expert], r_got
                        ).start()

                    @pl.when(jnp.logical_not(here))
                    def _():
                        reply(expert, width, side, block).start()

    relay(0)
    picks_t[...] = onehot[...].reshape(experts * slots, tokens).T
    relay(1)

    for lane in range(LANES):
        exchange(lane).wait_recv()
        mine = summed(q_part, q_recv, lane, h)
        query_out[:, lane * q_wide : (lane + 1) * q_wide] = mine + q_take[lane].astype(F32)
    gradient = query_out[...]
    weight = weight_v[...]
    count = 1.0 / weight.shape[1]
    radial = (jnp.sum(weight * gradient, axis=1, keepdims=True) * count) / (
        jnp.sum(weight * weight, axis=1, keepdims=True) * count + EPSILON
    )
    stepped = weight - STEP_RATE * (gradient - radial * weight)
    norm = jnp.sum(stepped * stepped, axis=1, keepdims=True) * count + EPSILON
    query_out[...] = stepped * lax.rsqrt(norm)

    for i in (4, 5):
        shares[i].wait_recv()
    produce(0, 0, 1, -1)
    produce(1, 0, 1, -1)
    relay(2, LONG)
    produce(0, 2, -2)
    produce(1, 2, -2)
    relay(2, SHORT)
    produce(0, 3, -3)
    produce(1, 3, -3)
    for copy in shares:
        copy.wait_send()
    for side in range(2):
        at = outgoing.at[side, pl.ds(0, 2 * NE - 2)]
        remote(at, at, disp_send.at[side], disp_recv.at[side], twin).wait_send()
    for recv, send, got in ((q_recv, q_send, q_got), (h_recv, h_send, h_got)):
        at = recv.at[:, pl.ds(0, NZ - 1)]
        remote(at, at, send, got.at[0, 0], twin).wait_send()
    for lane in range(LANES):
        exchange(lane).wait_send()

    for expert in range(2):
        relay(3, [chain for chain in LONG if chain[0] // 2 == expert])
        produce(expert, 4)

    remote(returned, returned, r_send, r_got, twin).wait_recv()
    moe_out[...] = sum(
        jnp.dot(
            picks_t[...],
            returned[half].reshape(experts * slots, -1),
            preferred_element_type=F32,
        )
        for half in range(2)
    )

    at = grads.at[:, :, pl.ds(0, NZ - 1)]
    remote(at, at, g_send, g_got.at[0, 0], twin).wait_send()
    at = result.at[pl.ds(0, result.shape[0] - 2)]
    remote(at, at, r_send, r_got, twin).wait_send()


def store_kernel(query_in, moe_in, query_out, moe_out):
    query_out[...] = query_in[...]
    moe_out[...] = moe_in[...]


def shards(
    attn_input,
    query_grad,
    query_weight,
    moe_cotangent,
    expert_ids,
    route_weights,
    gate_saved,
    up_saved,
    gate_weight,
    up_weight,
    down_weight,
):
    vmem = pl.BlockSpec(memory_space=pltpu.VMEM)
    hbm = pl.BlockSpec(memory_space=pl.ANY)
    dma = pltpu.SemaphoreType.DMA
    tokens, width = moe_cotangent.shape
    slots, local, hidden = gate_saved.shape
    rows, model = query_weight.shape
    batch, heads = query_grad.shape
    units = hidden // 2
    q_wide, h_wide = model // LANES, local * units // LANES
    scratch = [
        pltpu.VMEM(query_grad.shape, BF),
        pltpu.VMEM((heads, batch), BF),
        pltpu.VMEM(attn_input.shape, BF),
        pltpu.VMEM(query_weight.shape, F32),
        pltpu.VMEM((2, slots, local, units), BF),
        pltpu.VMEM((2, slots, local, units), BF),
        pltpu.VMEM((2, local, width, units), BF),
        pltpu.VMEM((2, local, width, units), BF),
        pltpu.VMEM((2, local, units, width), BF),
        pltpu.VMEM((tokens, width), BF),
        pltpu.VMEM((local * NE, slots, tokens), BF),
        pltpu.VMEM((tokens, local * NE * slots), BF),
        pltpu.VMEM((local * NE, slots, 1), F32),
        pltpu.VMEM((2, local * NE, slots, width), BF),
        pltpu.VMEM((2, local, NE, slots, width), BF),
        pltpu.VMEM((LANES, 2, NZ, rows, q_wide), BF),
        pltpu.VMEM((LANES, NZ, 2, rows, q_wide), BF),
        pltpu.VMEM((LANES, rows, q_wide), BF),
        pltpu.VMEM((LANES, rows, q_wide), BF),
        pltpu.VMEM((LANES, 2, NZ, slots, h_wide), BF),
        pltpu.VMEM((LANES, NZ, 2, slots, h_wide), BF),
        pltpu.VMEM((LANES, 2, NZ, slots, units), BF),
        pltpu.VMEM((local * 4 * NZ, slots, width), BF),
        pltpu.VMEM((2, NE, local, slots, width), BF),
        dma((11,)),
        dma((2,)),
        dma((2,)),
        dma((6,)),
        dma((6,)),
        dma,
        dma((LANES, NZ)),
        dma((LANES,)),
        dma((LANES,)),
        dma,
        dma((LANES, NZ)),
        dma,
        dma((LANES, NZ)),
        dma,
        dma,
    ]
    results = pl.pallas_call(
        step_kernel,
        name="backward_step",
        out_shape=(
            jax.ShapeDtypeStruct((rows, model), F32),
            jax.ShapeDtypeStruct((tokens, width), F32),
        ),
        in_specs=[vmem, vmem, vmem] + [hbm] * 8,
        out_specs=(vmem, vmem),
        scratch_shapes=scratch,
        compiler_params=pltpu.CompilerParams(
            collective_id=0, has_side_effects=True, vmem_limit_bytes=58 << 20
        ),
    )(
        expert_ids.T,
        route_weights.T,
        moe_cotangent,
        query_grad,
        attn_input,
        query_weight,
        gate_saved,
        up_saved,
        gate_weight,
        up_weight,
        down_weight.reshape(local, 2, units, width),
    )
    return pl.pallas_call(
        store_kernel,
        name="store_results",
        out_shape=tuple(jax.ShapeDtypeStruct(r.shape, r.dtype) for r in results),
        in_specs=[vmem] * 2,
        out_specs=(vmem, vmem),
    )(*results)


def solution(mesh):
    placed = (
        P("dp", None),
        P("dp", "expert"),
        P(("expert", "dp"), None),
        P("expert", "dp"),
        P("expert", None),
        P("expert", None),
        P("dp", "expert", None),
        P("dp", "expert", None),
        P("expert", "dp", None),
        P("expert", "dp", None),
        P("expert", None, "dp"),
    )
    return jax.shard_map(
        shards,
        mesh=mesh,
        in_specs=placed,
        out_specs=(P(("expert", "dp"), None), P("expert", "dp")),
        check_vma=False,
    )
```

```python
import functools

import jax
import jax.numpy as jnp
from jax import lax
from jax.experimental import pallas as pl
from jax.experimental.pallas import tpu as pltpu
from jax.sharding import PartitionSpec as P

STEP_RATE = 0.01
EPSILON = 1e-06
MESH = pl.DeviceIdType.MESH
NZ = 8
NE = 16
LANES = 4
LONG = ((0, 1, 4), (2, -1, 4), (1, 1, 4), (3, -1, 4))
SHORT = ((0, -1, 3), (2, 1, 3), (1, -1, 3), (3, 1, 3))
CHAINS = LONG + SHORT
NT = (((1,), (1,)), ((), ()))
BF = jnp.bfloat16
F32 = jnp.float32


def remote(src, dst, send_sem, recv_sem, device):
    return pltpu.make_async_remote_copy(
        src_ref=src,
        dst_ref=dst,
        send_sem=send_sem,
        recv_sem=recv_sem,
        device_id=device,
        device_id_type=MESH,
    )


def slot(way, t):
    return t if way > 0 else NZ // 2 + t


def step_kernel(
    ids_ref,
    route_ref,
    cot_ref,
    grad_hbm,
    input_hbm,
    weight_hbm,
    gate_hbm,
    up_hbm,
    gate_w_hbm,
    up_w_hbm,
    down_w_hbm,
    query_out,
    moe_out,
    grad_v,
    grad_t,
    input_v,
    weight_v,
    gate_v,
    up_v,
    gate_w,
    up_w,
    down_w,
    cot_in,
    onehot,
    picks_t,
    scale,
    outgoing,
    arrived,
    q_part,
    q_recv,
    q_give,
    q_take,
    h_part,
    h_recv,
    grads,
    result,
    returned,
    load_sem,
    disp_send,
    disp_recv,
    pair_send,
    pair_got,
    q_send,
    q_got,
    qx_send,
    qx_got,
    h_send,
    h_got,
    g_send,
    g_got,
    r_send,
    r_got,
):
    e = lax.axis_index("expert")
    d = lax.axis_index("dp")
    h = d // NZ
    z = lax.rem(d, NZ)
    twin_d = (1 - h) * NZ + z
    twin = (e, twin_d)
    ahead = (e, h * NZ + lax.rem(z + 1, NZ))
    behind = (e, h * NZ + lax.rem(z + NZ - 1, NZ))
    units = gate_w.shape[-1]
    slots = gate_v.shape[1]
    experts = 2 * NE
    tokens = ids_ref.shape[1]

    def toward(way):
        return ahead if way > 0 else behind

    def at_z(offset):
        return lax.rem(z + 2 * NZ + offset, NZ)

    own = pl.ds(pl.multiple_of(h * units, 128), units)
    other = pl.ds(pl.multiple_of((1 - h) * units, 128), units)
    q_wide = q_part.shape[-1]

    def strip(lane):
        at = pl.ds(lane * q_wide, q_wide)
        return (input_hbm.at[:, at], input_v.at[:, at])

    loads = [
        pltpu.make_async_copy(src, dst, load_sem.at[i])
        for i, (src, dst) in enumerate(
            (
                (grad_hbm, grad_v),
                strip(0),
                strip(2),
                strip(1),
                strip(3),
                (down_w_hbm.at[:, h], down_w.at[h]),
                (gate_hbm.at[:, :, own], gate_v.at[h]),
                (up_hbm.at[:, :, own], up_v.at[h]),
                (gate_w_hbm.at[:, :, own], gate_w.at[h]),
                (up_w_hbm.at[:, :, own], up_w.at[h]),
                (weight_hbm, weight_v),
            )
        )
    ]
    shares = [
        remote(src, dst, pair_send.at[i], pair_got.at[i], twin)
        for i, (src, dst) in enumerate(
            (
                (cot_ref, cot_in),
                (down_w_hbm.at[:, 1 - h], down_w.at[h]),
                (gate_hbm.at[:, :, other], gate_v.at[h]),
                (up_hbm.at[:, :, other], up_v.at[h]),
                (gate_w_hbm.at[:, :, other], gate_w.at[h]),
                (up_w_hbm.at[:, :, other], up_w.at[h]),
            )
        )
    ]
    for copy in loads:
        copy.start()

    barrier = pltpu.get_barrier_semaphore()

    for device in (twin, ahead, behind):
        pl.semaphore_signal(barrier, inc=1, device_id=device, device_id_type=MESH)

    @pl.loop(1, NE)
    def _(k):
        for column in (d, twin_d):
            pl.semaphore_signal(
                barrier, inc=1, device_id=(lax.rem(e + k, NE), column), device_id_type=MESH
            )

    which = lax.broadcasted_iota(jnp.int32, (experts, tokens), 0)
    chosen = jnp.zeros((experts, tokens), F32)
    share = jnp.zeros((experts, tokens), F32)
    for k in range(ids_ref.shape[0]):
        hit = ids_ref[k : k + 1, :] == which
        chosen = chosen + jnp.where(hit, 1.0, 0.0)
        share = share + jnp.where(hit, route_ref[k : k + 1, :], 0.0)
    earlier = lax.broadcasted_iota(jnp.int32, (tokens, tokens), 0) < lax.broadcasted_iota(
        jnp.int32, (tokens, tokens), 1
    )
    before = jnp.dot(
        chosen.astype(BF), jnp.where(earlier, 1.0, 0.0).astype(BF), preferred_element_type=F32
    )
    position = jnp.where(chosen > 0.5, before, -1.0).astype(jnp.int32)
    slot_iota = lax.broadcasted_iota(jnp.int32, (slots, tokens), 0)
    for block in range(experts):
        mine = position[block : block + 1, :] == slot_iota
        scale[block] = jnp.sum(
            jnp.where(mine, share[block : block + 1, :], 0.0), axis=1, keepdims=True
        )
        onehot[block] = jnp.where(mine, 1.0, 0.0).astype(BF)

    def fill(side, cot):
        group = 8
        for first in range(0, experts, group):
            picks = onehot[first : first + group].reshape(group * slots, tokens)
            rows = jnp.dot(picks, cot, preferred_element_type=F32)
            rows = rows * scale[first : first + group].reshape(group * slots, 1)
            outgoing[side, first : first + group] = rows.astype(BF).reshape(group, slots, -1)

    def dispatch(side, k):
        to = lax.rem(e + k, NE)
        return remote(
            outgoing.at[side, pl.ds(2 * to, 2)],
            arrived.at[side, :, e],
            disp_send.at[side],
            disp_recv.at[side],
            (to, d),
        )

    def dispatch_all(side):
        @pl.loop(1, NE)
        def _(k):
            dispatch(side, k).start()

        arrived[side, :, e] = outgoing[side, pl.ds(2 * e, 2)]

    def ring(part, recv, send, got, chain, t):
        lane, way, hops = chain
        src = part.at[lane, :, at_z(way * hops)] if t == 0 else recv.at[lane, slot(way, t - 1)]
        at = slot(way, t)
        return remote(src, recv.at[lane, at], send, got.at[lane, at], toward(way))

    def await_step(recv, send, got, chain, t):
        lane, way, _ = chain
        at = recv.at[lane, slot(way, t)]
        remote(at, at, send, got.at[lane, slot(way, t)], toward(way)).wait_recv()

    def begin(part, recv, send, got, lane):
        for chain in CHAINS:
            if chain[0] == lane:
                ring(part, recv, send, got, chain, 0).start()

    def forward(part, recv, send, got, t):
        for chain in CHAINS if t < 3 else LONG:
            lane, way, hops = chain
            await_step(recv, send, got, chain, t - 1)
            at = slot(way, t - 1)
            own_part = part[lane, :, at_z(way * (hops - t))]
            recv[lane, at] = (recv[lane, at].astype(F32) + own_part.astype(F32)).astype(BF)
            ring(part, recv, send, got, chain, t).start()

    def finish(recv, send, got, lane):
        for chain in CHAINS:
            if chain[0] == lane:
                await_step(recv, send, got, chain, chain[2] - 1)

    def summed(part, recv, lane, side):
        long = 1 if lane < 2 else -1
        both = recv[lane, slot(long, 3), side].astype(F32)
        both = both + recv[lane, slot(-long, 2), side].astype(F32)
        return both + part[lane, side, z].astype(F32)

    def q_forward(t):
        forward(q_part, q_recv, q_send, q_got, t)

    def h_forward(t):
        forward(h_part, h_recv, h_send, h_got, t)

    def q_product(lane):
        @pl.loop(0, q_wide // 256)
        def _(j):
            columns = pl.ds(pl.multiple_of(lane * q_wide + j * 256, 256), 256)
            part = jnp.dot(grad_t[...], input_v[:, columns], preferred_element_type=F32)
            q_part[lane, :, :, :, pl.ds(pl.multiple_of(j * 256, 256), 256)] = part.astype(
                BF
            ).reshape(2, NZ, 32, 256)

    loads[0].wait()
    grad_t[...] = grad_v[...].T
    loads[1].wait()
    q_product(0)

    pl.semaphore_wait(barrier, 2 * NE + 1)
    shares[0].start()
    begin(q_part, q_recv, q_send, q_got, 0)
    fill(h, cot_ref[...])
    dispatch_all(h)
    shares[1].start()
    loads[2].wait()
    q_product(2)
    begin(q_part, q_recv, q_send, q_got, 2)
    shares[0].wait_recv()
    fill(1 - h, cot_in[...])
    dispatch_all(1 - h)
    for i in (3, 4):
        loads[i].wait()
    for lane in (1, 3):
        q_product(lane)
        begin(q_part, q_recv, q_send, q_got, lane)

    q_forward(1)
    q_forward(2)
    shares[1].wait_recv()
    for copy in shares[2:]:
        copy.start()

    others = pl.ds(0, NE - 1)
    for side in range(2):
        at = arrived.at[side, :, others]
        remote(at, at, disp_send.at[side], disp_recv.at[side], twin).wait_recv()

    loads[5].wait()
    h_wide = h_part.shape[-1]
    for lane in range(LANES):
        expert, half = lane // 2, lane % 2
        rows = slice(half * h_wide, (half + 1) * h_wide)

        @pl.loop(0, 2)
        def _(block_side):
            part = 0.0
            for side in range(2):
                part = part + lax.dot_general(
                    arrived[side, expert, pl.ds(block_side * NZ, NZ)].reshape(NZ * slots, -1),
                    down_w[side, expert, rows, :],
                    NT,
                    preferred_element_type=F32,
                )
            h_part[lane, block_side] = part.astype(BF).reshape(NZ, slots, h_wide)

        begin(h_part, h_recv, h_send, h_got, lane)

    h_forward(1)
    q_forward(3)
    h_forward(2)
    h_forward(3)

    def gather(chain, t):
        lane, way, _ = chain
        at = grads.at[lane, :, at_z(-way * t)]
        return remote(at, at, g_send, g_got.at[lane, slot(way, t)], toward(way))

    for i in (6, 7, 8, 9, 10):
        loads[i].wait()
    for i in (2, 3):
        shares[i].wait_recv()
    for expert in range(2):
        for half in range(2):
            lane = 2 * expert + half
            finish(h_recv, h_send, h_got, lane)
            columns = slice(half * h_wide, (half + 1) * h_wide)
            for side in range(2):
                hidden = summed(h_part, h_recv, lane, side)
                g = gate_v[side, :, expert, columns].astype(F32)
                u = up_v[side, :, expert, columns].astype(F32)
                sigma = 1.0 / (1.0 + jnp.exp(-g))
                grads[2 * expert, side, z, :, columns] = (
                    hidden * u * sigma * (1.0 + g * (1.0 - sigma))
                ).astype(BF)
                grads[2 * expert + 1, side, z, :, columns] = (hidden * g * sigma).astype(BF)
        for chain in CHAINS:
            if chain[0] // 2 == expert:
                gather(chain, 0).start()

    def exchange(lane):
        return remote(q_give.at[lane], q_take.at[lane], qx_send.at[lane], qx_got.at[lane], twin)

    for lane in range(LANES):
        finish(q_recv, q_send, q_got, lane)
        q_give[lane] = summed(q_part, q_recv, lane, 1 - h).astype(BF)
        exchange(lane).start()

    def place(expert, width, side, block):
        return ((expert * 2 + width) * 2 + side) * NZ + block

    def reply(expert, width, side, block):
        return remote(
            result.at[place(expert, width, side, block)],
            returned.at[h, e, expert],
            r_send,
            r_got,
            (side * NZ + block, width * NZ + z),
        )

    def relay(t, chains=CHAINS):
        for chain in chains:
            gather(chain, t).wait_recv()
            if t + 1 < chain[2]:
                gather(chain, t + 1).start()

    def produce(expert, *offsets):
        blocks = [at_z(offset) for offset in offsets]

        def rows_of(lane):
            parts = [grads[lane, :, block].reshape(2 * slots, units) for block in blocks]
            return jnp.concatenate(parts, axis=0)

        gate, up = rows_of(2 * expert), rows_of(2 * expert + 1)
        for width in range(2):
            rows = lax.dot_general(gate, gate_w[width, expert], NT, preferred_element_type=F32)
            rows = rows + lax.dot_general(
                up, up_w[width, expert], NT, preferred_element_type=F32
            )
            rows = rows.astype(BF).reshape(len(blocks), 2, slots, -1)
            for i, block in enumerate(blocks):
                for side in range(2):
                    at = place(expert, width, side, block)
                    result[at] = rows[i, side]
                    here = (side * NZ + block == e) & (width == h)

                    @pl.when(here)
                    def _():
                        pltpu.make_async_copy(
                            result.at[at], returned.at[h, e, expert], r_got
                        ).start()

                    @pl.when(jnp.logical_not(here))
                    def _():
                        reply(expert, width, side, block).start()

    relay(0)
    picks_t[...] = onehot[...].reshape(experts * slots, tokens).T
    relay(1)

    for lane in range(LANES):
        exchange(lane).wait_recv()
        mine = summed(q_part, q_recv, lane, h)
        query_out[:, lane * q_wide : (lane + 1) * q_wide] = mine + q_take[lane].astype(F32)
    gradient = query_out[...]
    weight = weight_v[...]
    count = 1.0 / weight.shape[1]
    radial = (jnp.sum(weight * gradient, axis=1, keepdims=True) * count) / (
        jnp.sum(weight * weight, axis=1, keepdims=True) * count + EPSILON
    )
    stepped = weight - STEP_RATE * (gradient - radial * weight)
    norm = jnp.sum(stepped * stepped, axis=1, keepdims=True) * count + EPSILON
    query_out[...] = stepped * lax.rsqrt(norm)

    for i in (4, 5):
        shares[i].wait_recv()
    produce(0, 0, 1, -1)
    relay(2, LONG)
    produce(1, 0, 1, -1)
    produce(0, 2, -2)
    produce(1, 2, -2)
    relay(2, SHORT)
    produce(0, 3, -3)
    produce(1, 3, -3)
    for copy in shares:
        copy.wait_send()
    for side in range(2):
        at = outgoing.at[side, pl.ds(0, 2 * NE - 2)]
        remote(at, at, disp_send.at[side], disp_recv.at[side], twin).wait_send()
    for recv, send, got in ((q_recv, q_send, q_got), (h_recv, h_send, h_got)):
        at = recv.at[:, pl.ds(0, NZ - 1)]
        remote(at, at, send, got.at[0, 0], twin).wait_send()
    for lane in range(LANES):
        exchange(lane).wait_send()

    for expert in range(2):
        relay(3, [chain for chain in LONG if chain[0] // 2 == expert])
        produce(expert, 4)

    remote(returned, returned, r_send, r_got, twin).wait_recv()
    moe_out[...] = sum(
        jnp.dot(
            picks_t[...],
            returned[half].reshape(experts * slots, -1),
            preferred_element_type=F32,
        )
        for half in range(2)
    )

    at = grads.at[:, :, pl.ds(0, NZ - 1)]
    remote(at, at, g_send, g_got.at[0, 0], twin).wait_send()
    at = result.at[pl.ds(0, result.shape[0] - 2)]
    remote(at, at, r_send, r_got, twin).wait_send()


def store_kernel(query_in, moe_in, query_out, moe_out):
    query_out[...] = query_in[...]
    moe_out[...] = moe_in[...]


def shards(
    attn_input,
    query_grad,
    query_weight,
    moe_cotangent,
    expert_ids,
    route_weights,
    gate_saved,
    up_saved,
    gate_weight,
    up_weight,
    down_weight,
):
    vmem = pl.BlockSpec(memory_space=pltpu.VMEM)
    hbm = pl.BlockSpec(memory_space=pl.ANY)
    dma = pltpu.SemaphoreType.DMA
    tokens, width = moe_cotangent.shape
    slots, local, hidden = gate_saved.shape
    rows, model = query_weight.shape
    batch, heads = query_grad.shape
    units = hidden // 2
    q_wide, h_wide = model // LANES, local * units // LANES
    scratch = [
        pltpu.VMEM(query_grad.shape, BF),
        pltpu.VMEM((heads, batch), BF),
        pltpu.VMEM(attn_input.shape, BF),
        pltpu.VMEM(query_weight.shape, F32),
        pltpu.VMEM((2, slots, local, units), BF),
        pltpu.VMEM((2, slots, local, units), BF),
        pltpu.VMEM((2, local, width, units), BF),
        pltpu.VMEM((2, local, width, units), BF),
        pltpu.VMEM((2, local, units, width), BF),
        pltpu.VMEM((tokens, width), BF),
        pltpu.VMEM((local * NE, slots, tokens), BF),
        pltpu.VMEM((tokens, local * NE * slots), BF),
        pltpu.VMEM((local * NE, slots, 1), F32),
        pltpu.VMEM((2, local * NE, slots, width), BF),
        pltpu.VMEM((2, local, NE, slots, width), BF),
        pltpu.VMEM((LANES, 2, NZ, rows, q_wide), BF),
        pltpu.VMEM((LANES, NZ, 2, rows, q_wide), BF),
        pltpu.VMEM((LANES, rows, q_wide), BF),
        pltpu.VMEM((LANES, rows, q_wide), BF),
        pltpu.VMEM((LANES, 2, NZ, slots, h_wide), BF),
        pltpu.VMEM((LANES, NZ, 2, slots, h_wide), BF),
        pltpu.VMEM((LANES, 2, NZ, slots, units), BF),
        pltpu.VMEM((local * 4 * NZ, slots, width), BF),
        pltpu.VMEM((2, NE, local, slots, width), BF),
        dma((11,)),
        dma((2,)),
        dma((2,)),
        dma((6,)),
        dma((6,)),
        dma,
        dma((LANES, NZ)),
        dma((LANES,)),
        dma((LANES,)),
        dma,
        dma((LANES, NZ)),
        dma,
        dma((LANES, NZ)),
        dma,
        dma,
    ]
    results = pl.pallas_call(
        step_kernel,
        name="backward_step",
        out_shape=(
            jax.ShapeDtypeStruct((rows, model), F32),
            jax.ShapeDtypeStruct((tokens, width), F32),
        ),
        in_specs=[vmem, vmem, vmem] + [hbm] * 8,
        out_specs=(vmem, vmem),
        scratch_shapes=scratch,
        compiler_params=pltpu.CompilerParams(
            collective_id=0, has_side_effects=True, vmem_limit_bytes=58 << 20
        ),
    )(
        expert_ids.T,
        route_weights.T,
        moe_cotangent,
        query_grad,
        attn_input,
        query_weight,
        gate_saved,
        up_saved,
        gate_weight,
        up_weight,
        down_weight.reshape(local, 2, units, width),
    )
    return pl.pallas_call(
        store_kernel,
        name="store_results",
        out_shape=tuple(jax.ShapeDtypeStruct(r.shape, r.dtype) for r in results),
        in_specs=[vmem] * 2,
        out_specs=(vmem, vmem),
    )(*results)


def solution(mesh):
    placed = (
        P("dp", None),
        P("dp", "expert"),
        P(("expert", "dp"), None),
        P("expert", "dp"),
        P("expert", None),
        P("expert", None),
        P("dp", "expert", None),
        P("dp", "expert", None),
        P("expert", "dp", None),
        P("expert", "dp", None),
        P("expert", None, "dp"),
    )
    return jax.shard_map(
        shards,
        mesh=mesh,
        in_specs=placed,
        out_specs=(P(("expert", "dp"), None), P("expert", "dp")),
        check_vma=False,
    )
```
